512 devices in a mesh: samp: 128 (over z, y, core), cell: 4 (over x).
Axes of the slice: x: 4, y: 4, z: 16, core: 2. Of those that a mesh axis runs over, the one named last changes fastest.
Arguments:
- points: float32 [24, 262144], P(None, 'samp'), may hold values from -1 to 1
- yields: bfloat16 [262144, 1024], P('samp', 'cell'), may hold values from -6 to 6
- term_index: int32 [512, 2], replicated, may hold values from 0 to 95, as said below
- block_group: int32 [8], replicated, may hold values from 0 to 7
Outputs:
- coefficients: float32 [512, 1024], P('cell')
- sobol: float32 [8, 1024], P(None, 'cell')
The draws below stay inside these ranges and needn't reach their ends.
Inputs may be any that keep to these rules, and one draw needn't show every extreme that they name: `term_index`: row 0 is 0, 0 (the constant term); every other row names one parameter with degree 1 to 3 and column 0, or two different parameters with degrees 1 to 3 each, the lower column first; no two rows are the same.
All inputs are finite; a program needn't handle non-finite values.
Results may differ from the reference program's by a relative error of at most 0.0037.
Values sent between devices are 32-bit elements; how exact they have to be, the bound alone decides.
A program may use at most 64 MiB of HBM per device.

```python
import jax
import jax.numpy as jnp
import numpy as np
from jax import lax

PARAMS = 24
TERMS = 512
BLOCK = 64
GROUPS = 8
SAMP_DEV = 2048
BLOCKS = 8
CELLS = 1024
SAMPLES = 262144
N_SAMP = 128


def candidate_table():
    rows = []
    for param in range(23):
        for degree in range(1, 4):
            rows.append((4 * param + degree, 0))
    for degree in range(1, 3):
        rows.append((4 * 23 + degree, 0))
    for low in range(24):
        for high in range(low + 1, 24):
            for deg_low in range(1, 4):
                for deg_high in range(1, 4):
                    rows.append((4 * low + deg_low, 4 * high + deg_high))
    return np.array(rows, dtype=np.int32)


def draw_term_index(key, part):
    table = jnp.asarray(candidate_table())
    order = jax.random.permutation(jax.random.fold_in(key, 11), table.shape[0])
    chosen = table[order[:TERMS - 2]]
    head = jnp.array([[0, 0], [4 * PARAMS - 1, 0]], dtype=jnp.int32)
    return jnp.concatenate([head, chosen], axis=0).astype(jnp.int32)


def set_ends(values, key, smallest, high):
    extent = values.shape
    place = [jax.random.randint(jax.random.fold_in(key, axis), (), 0, extent[axis]) for axis in range(len(extent))]
    values = values.at[tuple(place)].set(smallest)
    longest = extent.index(max(extent))
    place[longest] = (place[longest] + 1) % extent[longest]
    return values.at[tuple(place)].set(high)


def block_levels(own_key, extent, cuts, smallest, high):
    gain = 1.0
    for position, blocks in cuts:
        steps = jax.random.uniform(jax.random.fold_in(jax.random.fold_in(own_key, 6), position), (blocks,), jnp.float32, smallest / len(cuts), high / len(cuts))
        gain = gain * jnp.repeat(jnp.exp(steps), extent[position] // blocks).reshape((-1,) + (1,) * (len(extent) - 1 - position))
    return gain


def scatter_about(stream_key, extent, scale, limit, cuts=(), kind=jnp.bfloat16):
    factor_of = block_levels(stream_key, extent, cuts, -0.22, 0.18) if cuts else 1.0
    values = jax.random.normal(stream_key, extent, jnp.float32) * scale * factor_of
    return jnp.minimum(jnp.maximum(values, -limit), limit).astype(kind)


def setup_inputs(seed: int = 0) -> dict:
    splits = jax.random.split(jax.random.key(seed), 5)
    points = jnp.clip(jax.random.uniform(splits[0], (PARAMS, SAMPLES), jnp.float32, -1.0, 1.0) * block_levels(splits[0], (PARAMS, SAMPLES), ((1, 128),), -0.4, 0.0), -1.0, 1.0)
    yields = scatter_about(splits[1], (SAMPLES, CELLS), 1.0, 6.0, ((0, 128), (1, 4)))
    term_index = draw_term_index(jax.random.fold_in(splits[4], 71), 0)
    block_group = set_ends(jax.random.randint(splits[3], (BLOCKS,), 0, GROUPS), jax.random.fold_in(splits[3], 1), 0, GROUPS - 1).astype(jnp.int32)
    return {"points": points, "yields": yields, "term_index": term_index, "block_group": block_group}


def basis_rows(xs):
    ones = jnp.ones_like(xs)
    first = 1.7320508075688772 * xs
    second = 2.23606797749979 * (1.5 * xs * xs - 0.5)
    third = 2.6457513110645907 * (2.5 * xs * xs * xs - 1.5 * xs)
    stacked = jnp.stack([ones, first, second, third], axis=1)
    return stacked.reshape(4 * xs.shape[0], xs.shape[1])

def design(xs, term_index):
    table = basis_rows(xs)
    columns = jnp.arange(table.shape[0], dtype=jnp.int32)
    pick_a = (term_index[:, 0:1] == columns[None, :]).astype(table.dtype)
    pick_b = (term_index[:, 1:2] == columns[None, :]).astype(table.dtype)
    left = jnp.dot(pick_a, table, precision=lax.Precision.HIGHEST)
    right = jnp.dot(pick_b, table, precision=lax.Precision.HIGHEST)
    return (left * right).astype(jnp.bfloat16)

def reference(points, yields, term_index, block_group):
    xb = points.reshape(PARAMS, N_SAMP, SAMP_DEV).transpose(1, 0, 2)
    yb = yields.reshape(N_SAMP, SAMP_DEV, CELLS)

    def accumulate(carry, item):
        gram, cross = carry
        xs, ys = item
        psi = design(xs, term_index)
        gram = gram + jnp.dot(psi.astype(jnp.float32), psi.T.astype(jnp.float32), preferred_element_type=jnp.float32)
        cross = cross + jnp.dot(psi.astype(jnp.float32), ys.astype(jnp.float32), preferred_element_type=jnp.float32)
        return ((gram, cross), None)
    start = (jnp.zeros((TERMS, TERMS), jnp.float32), jnp.zeros((TERMS, CELLS), jnp.float32))
    (gram, cross), unused = lax.scan(accumulate, start, (xb, yb))
    lower = jnp.linalg.cholesky(gram)
    inner = lax.linalg.triangular_solve(lower, cross, left_side=True, lower=True)
    coef = lax.linalg.triangular_solve(lower, inner, left_side=True, lower=True, transpose_a=True)
    coefficients = coef * jnp.sqrt(jnp.float32(SAMPLES))
    keep = (jnp.arange(TERMS) >= 1).astype(jnp.float32)
    squares = coef * coef * keep[:, None]
    groups = jnp.repeat(block_group, BLOCK)
    member = (groups[None, :] == jnp.arange(GROUPS, dtype=jnp.int32)[:, None]).astype(jnp.float32)
    part = jnp.dot(member, squares, precision=lax.Precision.HIGHEST)
    total = lax.optimization_barrier(jnp.sum(squares, axis=0))
    return (coefficients, part / total[None, :])
```

```python
import jax
import jax.numpy as jnp
from jax import lax
from jax.experimental import pallas as pl
from jax.experimental.pallas import tpu as pltpu
from jax.sharding import PartitionSpec as P

BLOCK = 64
GROUPS = 8
TERMS = 512
MESH = pl.DeviceIdType.MESH
F32 = jnp.float32
BF16 = jnp.bfloat16


def local_kernel(points_ref, yields_ref, term_ref, cross_ref, gram_ref, psi_ref):
    params, samples = points_ref.shape
    width = 3 * params
    lane = lax.broadcasted_iota(jnp.int32, (TERMS, 256), 1)

    def pick(column):
        degree = column & 3
        target = (degree - 1) * params + (column >> 2)
        hit = (lane == target) | (lane == target + width) | (lane == target + 2 * width)
        chosen = jnp.where(degree == 0, (lane == 3 * width).astype(F32), hit.astype(F32))
        return chosen.astype(BF16)

    pick_a = pick(term_ref[:, 0:1])
    pick_b = pick(term_ref[:, 1:2])
    step = 512
    for start in range(0, samples, step):
        xs = points_ref[:, start:start + step]
        first = 1.7320508075688772 * xs
        second = 2.23606797749979 * (1.5 * xs * xs - 0.5)
        third = 2.6457513110645907 * (2.5 * xs * xs * xs - 1.5 * xs)
        degrees = jnp.concatenate([first, second, third], axis=0)
        high = degrees.astype(BF16).astype(F32)
        rest = degrees - high
        middle = rest.astype(BF16).astype(F32)
        low = rest - middle
        table = jnp.concatenate(
            [high, middle, low, jnp.ones((8, step), F32), jnp.zeros((256 - 3 * width - 8, step), F32)], axis=0
        ).astype(BF16)
        left = jnp.dot(pick_a, table, preferred_element_type=F32)
        right = jnp.dot(pick_b, table, preferred_element_type=F32)
        psi_ref[:, start:start + step] = (left * right).astype(BF16)

    cross_ref[...] = jnp.dot(psi_ref[...], yields_ref[...], preferred_element_type=F32)

    cell = lax.axis_index("cell")
    low_half = cell < 2
    spots = (
        (0, 128, cell * 128, cell * 128),
        (128, 128, cell * 128, lax.rem(cell + 1, 4) * 128),
        (256, 64, jnp.where(low_half, cell * 128, cell * 128 - 192), jnp.where(low_half, cell * 128 + 256, cell * 128)),
    )
    for place, rows, a, b in spots:
        one = psi_ref[pl.ds(pl.multiple_of(a, 64), rows), :]
        two = psi_ref[pl.ds(pl.multiple_of(b, 128), 128), :]
        gram_ref[place:place + rows, :] = lax.dot_general(one, two, (((1,), (1,)), ((), ())), preferred_element_type=F32)


def local_products(points, yields, term_index):
    vmem = pl.BlockSpec(memory_space=pltpu.VMEM)
    return pl.pallas_call(
        local_kernel,
        out_shape=(jax.ShapeDtypeStruct((TERMS, yields.shape[1]), F32), jax.ShapeDtypeStruct((320, 128), F32)),
        in_specs=[vmem] * 3,
        out_specs=(vmem, vmem),
        scratch_shapes=[pltpu.VMEM((TERMS, points.shape[1]), BF16)],
        compiler_params=pltpu.CompilerParams(vmem_limit_bytes=48 << 20),
        name="local_products",
    )(points, yields, term_index)


def sum_kernel(cross_ref, gram_ref, cross_out, gram_out, r_core, s_core, r_y, s_y, r_zc, r_zg, a_z, send_sem, recv_sem):
    samp, cell = lax.axis_index("samp"), lax.axis_index("cell")
    core = lax.rem(samp, 2)
    y = lax.rem(samp // 2, 4)
    z = samp // 8

    def at(zz, yy, cc):
        return {"samp": (zz * 4 + yy) * 2 + cc, "cell": cell}

    def along_x(d):
        return {"samp": samp, "cell": lax.rem(cell + d, 4)}

    other = at(z, y, 1 - core)
    ys = [lax.rem(y + d, 4) for d in range(1, 4)]
    zs = [lax.rem(z + d, 16) for d in range(1, 16)]
    barrier = pltpu.get_barrier_semaphore()
    everyone = [other] + [at(z, v, core) for v in ys] + [at(v, y, core) for v in zs] + [along_x(d) for d in range(1, 4)]
    for device in everyone:
        pl.semaphore_signal(barrier, inc=1, device_id=device, device_id_type=MESH)
    pl.semaphore_wait(barrier, len(everyone))

    count = [0]
    started = []

    def send(src, dst, device):
        n = count[0]
        count[0] += 1
        copy = pltpu.make_async_remote_copy(
            src_ref=src, dst_ref=dst, send_sem=send_sem.at[n], recv_sem=recv_sem.at[n], device_id=device, device_id_type=MESH
        )
        return copy

    def go(src, dst, device):
        copy = send(src, dst, device)
        copy.start()
        started.append(copy)
        return copy

    far = pl.multiple_of((1 - core) * 128, 128)
    near = pl.multiple_of(core * 128, 128)
    first = []
    for q in range(4):
        first.append((
            go(cross_ref.at[q * 128:(q + 1) * 128, pl.ds(far, 128)], r_core.at[q, 0:128], other),
            go(gram_ref.at[pl.ds(pl.multiple_of((1 - core) * 160 + q * 40, 8), 40)], r_core.at[q, 128:168], other),
        ))
    for q in range(4):
        for copy in first[q]:
            copy.wait_recv()
        s_core[q, 0:128] = cross_ref[q * 128:(q + 1) * 128, pl.ds(near, 128)] + r_core[q, 0:128]
        s_core[q, 128:168] = gram_ref[pl.ds(pl.multiple_of(core * 160 + q * 40, 8), 40)] + r_core[q, 128:168]

    second = [go(s_core.at[v], r_y.at[d], at(z, v, core)) for d, v in enumerate(ys)]
    for copy in second:
        copy.wait_recv()
    s_y[...] = (s_core[y] + r_y[0]) + (r_y[1] + r_y[2])

    third = []
    extra = []
    for d, v in enumerate(zs):
        third.append(go(s_y.at[pl.ds(pl.multiple_of(v * 8, 8), 8)], r_zc.at[d], at(v, y, core)))
        copy = send(s_y.at[pl.ds(pl.multiple_of(128 + jnp.minimum(v, 4) * 8, 8), 8)], r_zg.at[d], at(v, y, core))
        extra.append(copy)
        pl.when(v < 5)(copy.start)
    for copy in third:
        copy.wait_recv()
    mine = pl.ds(pl.multiple_of(z * 8, 8), 8)
    total = s_y[mine]
    for d in range(15):
        total = total + r_zc[d]
    a_z[mine] = total
    fourth = [go(a_z.at[mine], a_z.at[mine], at(v, y, core)) for v in zs]
    mine_gram = pl.ds(pl.multiple_of(128 + jnp.minimum(z, 4) * 8, 8), 8)
    fourth_gram = [send(a_z.at[mine_gram], a_z.at[mine_gram], at(v, y, core)) for v in zs]

    @pl.when(z < 5)
    def _():
        for copy in extra:
            copy.wait_recv()
        total = s_y[mine_gram]
        for d in range(15):
            total = total + r_zg[d]
        a_z[mine_gram] = total
        for copy in fourth_gram:
            copy.start()

    for copy in fourth:
        copy.wait_recv()
    for d, copy in enumerate(fourth_gram):
        pl.when(lax.rem(z + 15 - d, 16) < 5)(copy.wait_recv)

    fifth = []
    cross_out[pl.ds(pl.multiple_of(y * 128, 128), 128), pl.ds(near, 128)] = a_z[0:128]
    gram_out[cell, pl.ds(pl.multiple_of(core * 160 + y * 40, 8), 40)] = a_z[128:168]
    for v in ys:
        fifth.append((
            go(a_z.at[128:168], gram_out.at[cell, pl.ds(pl.multiple_of(core * 160 + y * 40, 8), 40)], at(z, v, core)),
            go(a_z.at[0:128], cross_out.at[pl.ds(pl.multiple_of(y * 128, 128), 128), pl.ds(near, 128)], at(z, v, core)),
        ))
    for gram_copy, unused in fifth:
        gram_copy.wait_recv()
    half = pl.ds(pl.multiple_of(core * 160, 8), 160)
    sixth = [go(gram_out.at[cell, half], gram_out.at[cell, half], along_x(d)) for d in range(1, 4)]
    for unused, cross_copy in fifth:
        cross_copy.wait_recv()
    seventh = [go(cross_out.at[:, pl.ds(near, 128)], cross_out.at[:, pl.ds(near, 128)], other)]
    for copy in sixth:
        copy.wait_recv()
    seventh.append(go(gram_out.at[:, half], gram_out.at[:, half], other))
    for copy in seventh:
        copy.wait_recv()
    for copy in started:
        copy.wait_send()
    for d, v in enumerate(zs):
        pl.when(v < 5)(extra[d].wait_send)

    @pl.when(z < 5)
    def _():
        for copy in fourth_gram:
            copy.wait_send()


def sum_all(cross, gram):
    vmem = pl.BlockSpec(memory_space=pltpu.VMEM)
    copies = 8 + 3 + 30 + 30 + 6 + 3 + 2
    return pl.pallas_call(
        sum_kernel,
        out_shape=(jax.ShapeDtypeStruct(cross.shape, F32), jax.ShapeDtypeStruct((4, 320, 128), F32)),
        in_specs=[vmem] * 2,
        out_specs=(vmem, vmem),
        scratch_shapes=[
            pltpu.VMEM((4, 168, 128), F32),
            pltpu.VMEM((4, 168, 128), F32),
            pltpu.VMEM((3, 168, 128), F32),
            pltpu.VMEM((168, 128), F32),
            pltpu.VMEM((15, 8, 128), F32),
            pltpu.VMEM((15, 8, 128), F32),
            pltpu.VMEM((168, 128), F32),
            pltpu.SemaphoreType.DMA((copies,)),
            pltpu.SemaphoreType.DMA((copies,)),
        ],
        compiler_params=pltpu.CompilerParams(collective_id=0, has_side_effects=True, vmem_limit_bytes=32 << 20),
        name="sum_all",
    )(cross, gram)


def whole_gram(parts):
    diag = [parts[i, 0:128] for i in range(4)]
    next_one = [parts[i, 128:256] for i in range(4)]
    skip = [jnp.concatenate([parts[i, 256:320], parts[i + 2, 256:320]], axis=0) for i in range(2)]
    return jnp.block([
        [diag[0], next_one[0], skip[0], next_one[3].T],
        [next_one[0].T, diag[1], next_one[1], skip[1]],
        [skip[0].T, next_one[1].T, diag[2], next_one[2]],
        [next_one[3], skip[1].T, next_one[2].T, diag[3]],
    ])


def on_device(points, yields, term_index, block_group):
    cross_local, gram_local = local_products(points, yields, term_index)
    cross, gram_parts = sum_all(cross_local, gram_local)
    gram = whole_gram(gram_parts)
    lower = jnp.linalg.cholesky(gram)
    inner = lax.linalg.triangular_solve(lower, cross, left_side=True, lower=True)
    coef = lax.linalg.triangular_solve(lower, inner, left_side=True, lower=True, transpose_a=True)
    total_samples = points.shape[1] * lax.axis_size("samp")
    scaled = coef * jnp.sqrt(jnp.float32(total_samples))
    terms = coef.shape[0]
    keep = (jnp.arange(terms) >= 1).astype(jnp.float32)
    squares = coef * coef * keep[:, None]
    groups = jnp.repeat(block_group, BLOCK)
    member = (groups[None, :] == jnp.arange(GROUPS, dtype=jnp.int32)[:, None]).astype(jnp.float32)
    part = jnp.dot(member, squares, precision=lax.Precision.HIGHEST)
    total = jnp.sum(squares, axis=0)
    sobol = part / total[None, :]
    coefficients = lax.all_to_all(scaled, "cell", split_axis=0, concat_axis=1, tiled=True)
    return (coefficients, sobol)


def solution(mesh):
    placed = (P(None, "samp"), P("samp", "cell"), P(), P())
    return jax.shard_map(
        on_device,
        mesh=mesh,
        in_specs=placed,
        out_specs=(P("cell", None), P(None, "cell")),
        check_vma=False,
    )
```

```python
import functools

import jax
import jax.numpy as jnp
from jax import lax
from jax.experimental import pallas as pl
from jax.experimental.pallas import tpu as pltpu
from jax.sharding import PartitionSpec as P

GROUPS = 8
TERMS = 512
HI = lax.Precision.HIGHEST
MESH = pl.DeviceIdType.MESH
F32 = jnp.float32
BF16 = jnp.bfloat16


def local_kernel(points_ref, yields_ref, term_ref, cross_ref, gram_ref, psi_ref):
    params, samples = points_ref.shape
    width = 3 * params
    lane = lax.broadcasted_iota(jnp.int32, (TERMS, 256), 1)

    def pick(column):
        degree = column & 3
        target = (degree - 1) * params + (column >> 2)
        hit = (lane == target) | (lane == target + width) | (lane == target + 2 * width)
        chosen = jnp.where(degree == 0, (lane == 3 * width).astype(F32), hit.astype(F32))
        return chosen.astype(BF16)

    pick_a = pick(term_ref[:, 0:1])
    pick_b = pick(term_ref[:, 1:2])
    step = 512
    for start in range(0, samples, step):
        xs = points_ref[:, start:start + step]
        first = 1.7320508075688772 * xs
        second = 2.23606797749979 * (1.5 * xs * xs - 0.5)
        third = 2.6457513110645907 * (2.5 * xs * xs * xs - 1.5 * xs)
        degrees = jnp.concatenate([first, second, third], axis=0)
        high = degrees.astype(BF16).astype(F32)
        rest = degrees - high
        middle = rest.astype(BF16).astype(F32)
        low = rest - middle
        table = jnp.concatenate(
            [high, middle, low, jnp.ones((8, step), F32), jnp.zeros((256 - 3 * width - 8, step), F32)], axis=0
        ).astype(BF16)
        left = jnp.dot(pick_a, table, preferred_element_type=F32)
        right = jnp.dot(pick_b, table, preferred_element_type=F32)
        psi_ref[:, start:start + step] = (left * right).astype(BF16)

    cross_ref[...] = jnp.dot(psi_ref[...], yields_ref[...], preferred_element_type=F32)

    cell = lax.axis_index("cell")
    low_half = cell < 2
    spots = (
        (0, 128, cell * 128, cell * 128),
        (128, 128, jnp.where(cell == 3, 0, cell * 128), jnp.minimum(cell + 1, 3) * 128),
        (256, 64, jnp.where(low_half, cell * 128, cell * 128 - 192), jnp.where(low_half, cell * 128 + 256, cell * 128)),
    )
    for place, rows, a, b in spots:
        one = psi_ref[pl.ds(pl.multiple_of(a, 64), rows), :]
        two = psi_ref[pl.ds(pl.multiple_of(b, 128), 128), :]
        gram_ref[place:place + rows, :] = lax.dot_general(one, two, (((1,), (1,)), ((), ())), preferred_element_type=F32)


def local_products(points, yields, term_index):
    vmem = pl.BlockSpec(memory_space=pltpu.VMEM)
    return pl.pallas_call(
        local_kernel,
        out_shape=(jax.ShapeDtypeStruct((TERMS, yields.shape[1]), F32), jax.ShapeDtypeStruct((320, 128), F32)),
        in_specs=[vmem] * 3,
        out_specs=(vmem, vmem),
        scratch_shapes=[pltpu.VMEM((TERMS, points.shape[1]), BF16)],
        compiler_params=pltpu.CompilerParams(vmem_limit_bytes=48 << 20),
        name="local_products",
    )(points, yields, term_index)


def sum_kernel(cross_ref, gram_ref, cross_out, gram_out, r_core, s_core, r_y, s_y, r_zc, r_zg, a_z, send_sem, recv_sem):
    samp, cell = lax.axis_index("samp"), lax.axis_index("cell")
    core = lax.rem(samp, 2)
    y = lax.rem(samp // 2, 4)
    z = samp // 8

    def at(zz, yy, cc):
        return {"samp": (zz * 4 + yy) * 2 + cc, "cell": cell}

    def along_x(d):
        return {"samp": samp, "cell": lax.rem(cell + d, 4)}

    other = at(z, y, 1 - core)
    ys = [lax.rem(y + d, 4) for d in range(1, 4)]
    zs = [lax.rem(z + d, 16) for d in range(1, 16)]
    barrier = pltpu.get_barrier_semaphore()
    everyone = [other] + [at(z, v, core) for v in ys] + [at(v, y, core) for v in zs] + [along_x(d) for d in range(1, 4)]
    for device in everyone:
        pl.semaphore_signal(barrier, inc=1, device_id=device, device_id_type=MESH)
    pl.semaphore_wait(barrier, len(everyone))

    count = [0]
    started = []

    def send(src, dst, device):
        n = count[0]
        count[0] += 1
        copy = pltpu.make_async_remote_copy(
            src_ref=src, dst_ref=dst, send_sem=send_sem.at[n], recv_sem=recv_sem.at[n], device_id=device, device_id_type=MESH
        )
        return copy

    def go(src, dst, device):
        copy = send(src, dst, device)
        copy.start()
        started.append(copy)
        return copy

    far = pl.multiple_of((1 - core) * 128, 128)
    near = pl.multiple_of(core * 128, 128)
    first = []
    for q in range(4):
        first.append((
            go(cross_ref.at[q * 128:(q + 1) * 128, pl.ds(far, 128)], r_core.at[q, 0:128], other),
            go(gram_ref.at[pl.ds(pl.multiple_of((1 - core) * 160 + q * 40, 8), 40)], r_core.at[q, 128:168], other),
        ))
    for q in range(4):
        for copy in first[q]:
            copy.wait_recv()
        s_core[q, 0:128] = cross_ref[q * 128:(q + 1) * 128, pl.ds(near, 128)] + r_core[q, 0:128]
        s_core[q, 128:168] = gram_ref[pl.ds(pl.multiple_of(core * 160 + q * 40, 8), 40)] + r_core[q, 128:168]

    second = [go(s_core.at[v], r_y.at[d], at(z, v, core)) for d, v in enumerate(ys)]
    for copy in second:
        copy.wait_recv()
    s_y[...] = (s_core[y] + r_y[0]) + (r_y[1] + r_y[2])

    third = []
    extra = []
    for d, v in enumerate(zs):
        third.append(go(s_y.at[pl.ds(pl.multiple_of(v * 8, 8), 8)], r_zc.at[d], at(v, y, core)))
        copy = send(s_y.at[pl.ds(pl.multiple_of(128 + jnp.minimum(v, 4) * 8, 8), 8)], r_zg.at[d], at(v, y, core))
        extra.append(copy)
        pl.when(v < 5)(copy.start)
    for copy in third:
        copy.wait_recv()
    mine = pl.ds(pl.multiple_of(z * 8, 8), 8)
    total = s_y[mine]
    for d in range(15):
        total = total + r_zc[d]
    a_z[mine] = total
    fourth = [go(a_z.at[mine], a_z.at[mine], at(v, y, core)) for v in zs]
    mine_gram = pl.ds(pl.multiple_of(128 + jnp.minimum(z, 4) * 8, 8), 8)
    fourth_gram = [send(a_z.at[mine_gram], a_z.at[mine_gram], at(v, y, core)) for v in zs]

    @pl.when(z < 5)
    def _():
        for copy in extra:
            copy.wait_recv()
        total = s_y[mine_gram]
        for d in range(15):
            total = total + r_zg[d]
        a_z[mine_gram] = total
        for copy in fourth_gram:
            copy.start()

    for copy in fourth:
        copy.wait_recv()
    for d, copy in enumerate(fourth_gram):
        pl.when(lax.rem(z + 15 - d, 16) < 5)(copy.wait_recv)

    fifth = []
    cross_out[pl.ds(pl.multiple_of(y * 128, 128), 128), pl.ds(near, 128)] = a_z[0:128]
    gram_out[cell, pl.ds(pl.multiple_of(core * 160 + y * 40, 8), 40)] = a_z[128:168]
    for v in ys:
        fifth.append((
            go(a_z.at[128:168], gram_out.at[cell, pl.ds(pl.multiple_of(core * 160 + y * 40, 8), 40)], at(z, v, core)),
            go(a_z.at[0:128], cross_out.at[pl.ds(pl.multiple_of(y * 128, 128), 128), pl.ds(near, 128)], at(z, v, core)),
        ))
    for gram_copy, unused in fifth:
        gram_copy.wait_recv()
    half = pl.ds(pl.multiple_of(core * 160, 8), 160)
    sixth = [go(gram_out.at[cell, half], gram_out.at[cell, half], along_x(d)) for d in range(1, 4)]
    for unused, cross_copy in fifth:
        cross_copy.wait_recv()
    seventh = [go(cross_out.at[:, pl.ds(near, 128)], cross_out.at[:, pl.ds(near, 128)], other)]
    for copy in sixth:
        copy.wait_recv()
    seventh.append(go(gram_out.at[:, half], gram_out.at[:, half], other))
    for copy in seventh:
        copy.wait_recv()
    for copy in started:
        copy.wait_send()
    for d, v in enumerate(zs):
        pl.when(v < 5)(extra[d].wait_send)

    @pl.when(z < 5)
    def _():
        for copy in fourth_gram:
            copy.wait_send()


def sum_all(cross, gram):
    vmem = pl.BlockSpec(memory_space=pltpu.VMEM)
    copies = 8 + 3 + 30 + 30 + 6 + 3 + 2
    return pl.pallas_call(
        sum_kernel,
        out_shape=(jax.ShapeDtypeStruct(cross.shape, F32), jax.ShapeDtypeStruct((4, 320, 128), F32)),
        in_specs=[vmem] * 2,
        out_specs=(vmem, vmem),
        scratch_shapes=[
            pltpu.VMEM((4, 168, 128), F32),
            pltpu.VMEM((4, 168, 128), F32),
            pltpu.VMEM((3, 168, 128), F32),
            pltpu.VMEM((168, 128), F32),
            pltpu.VMEM((15, 8, 128), F32),
            pltpu.VMEM((15, 8, 128), F32),
            pltpu.VMEM((168, 128), F32),
            pltpu.SemaphoreType.DMA((copies,)),
            pltpu.SemaphoreType.DMA((copies,)),
        ],
        compiler_params=pltpu.CompilerParams(collective_id=0, has_side_effects=True, vmem_limit_bytes=32 << 20),
        name="sum_all",
    )(cross, gram)


def full(row):
    return jnp.broadcast_to(row, (8, 128))


def sweep_rows(rows, p, lane, sub):
    pivot = rows[p]
    at = 8 * p
    inside = (lane >= at) & (lane < at + 8)
    spread = [full(pivot[:, at + j:at + j + 1]) for j in range(8)]
    m = [[None] * 8 for _ in range(8)]
    for j in range(8):
        for i in range(j + 1):
            m[i][j] = full(spread[j][i:i + 1, :])
    for k in range(8):
        r = 1.0 / m[k][k]
        t = [None if j == k else m[min(j, k)][max(j, k)] * r for j in range(8)]
        old = [m[min(j, k)][max(j, k)] for j in range(8)]
        for j in range(8):
            for i in range(j + 1):
                if i != k and j != k:
                    m[i][j] = m[i][j] - old[i] * t[j]
        for j in range(8):
            if j != k:
                m[min(j, k)][max(j, k)] = t[j]
        m[k][k] = -r
    target = jnp.where(inside, jnp.where(lane - at == sub, 1.0, 0.0), -pivot)
    source = [full(target[i:i + 1, :]) for i in range(8)]
    wide = []
    for j in range(8):
        terms = [m[min(i, j)][max(i, j)] * source[i] for i in range(8)]
        wide.append(((terms[0] + terms[1]) + (terms[2] + terms[3])) + ((terms[4] + terms[5]) + (terms[6] + terms[7])))
    out = [None] * 16
    order = [(p + 1 + q) % 16 for q in range(15)]
    for q in order:
        terms = [full(rows[q][:, at + j:at + j + 1]) * wide[j] for j in range(8)]
        total = ((terms[0] + terms[1]) + (terms[2] + terms[3])) + ((terms[4] + terms[5]) + (terms[6] + terms[7]))
        out[q] = jnp.where(inside, 0.0, rows[q]) - total
    packed = wide[7]
    for j in range(7):
        packed = jnp.where(sub == j, wide[j], packed)
    out[p] = packed
    return out


def solve_kernel(scale, cross_ref, gram_ref, group_ref, coef_ref, sobol_ref, a_ref, d_ref):
    cells = cross_ref.shape[1]
    lane = lax.broadcasted_iota(jnp.int32, (8, 128), 1)
    sub = lax.broadcasted_iota(jnp.int32, (8, 128), 0)
    for b in range(4):
        a_ref[b, :, 128 * b:128 * b + 128] = gram_ref[b, 0:128]
        a_ref[b, :, 512:512 + cells] = cross_ref[128 * b:128 * b + 128]
    for b in range(3):
        a_ref[b, :, 128 * b + 128:128 * b + 256] = gram_ref[b, 128:256]
    a_ref[0, :, 384:512] = gram_ref[3, 128:256]
    for b in range(2):
        a_ref[b, 0:64, 128 * b + 256:128 * b + 384] = gram_ref[b, 256:320]
        a_ref[b, 64:128, 128 * b + 256:128 * b + 384] = gram_ref[b + 2, 256:320]
    end = 512 + cells
    d_ref[...] = a_ref[0, :, 0:128]

    def block(b, unused):
        rows = [d_ref[8 * i:8 * i + 8, :] for i in range(16)]
        for p in range(16):
            rows = sweep_rows(rows, p, lane, sub)
        for i in range(16):
            d_ref[8 * i:8 * i + 8, :] = -rows[i]
        for s in range(4):
            @pl.when(b == s)
            def _():
                begin = 128 * s + 128
                w = jnp.dot(d_ref[...], a_ref[s, :, begin:end], precision=HI, preferred_element_type=F32)
                for i in range(s + 1, 4):
                    here = slice(128 * i, end)
                    a_ref[i, :, here] -= lax.dot_general(
                        a_ref[s, :, 128 * i:128 * i + 128], w[:, 128 * i - begin:], (((0,), (0,)), ((), ())), precision=HI, preferred_element_type=F32)
                a_ref[s, :, begin:end] = w
                if s < 3:
                    d_ref[...] = a_ref[s + 1, :, begin:begin + 128]
        return unused

    lax.fori_loop(0, 4, block, 0)
    found = [None] * 4
    for b in (3, 2, 1, 0):
        x = a_ref[b, :, 512:end]
        if b < 3:
            below = jnp.concatenate(found[b + 1:], axis=0)
            x = x - jnp.dot(a_ref[b, :, 128 * b + 128:512], below, precision=HI, preferred_element_type=F32)
        found[b] = x
    sums = []
    for b in range(4):
        x = found[b]
        coef_ref[128 * b:128 * b + 128] = x * scale
        sq = x * x
        if b == 0:
            sq = jnp.where(lax.broadcasted_iota(jnp.int32, sq.shape, 0) == 0, 0.0, sq)
        sums.append(jnp.sum(sq[0:64], axis=0, keepdims=True))
        sums.append(jnp.sum(sq[64:128], axis=0, keepdims=True))
    total = sums[0]
    for s in sums[1:]:
        total = total + s
    for g in range(GROUPS):
        part = jnp.zeros_like(total)
        for b in range(8):
            part = part + jnp.where(group_ref[b] == g, sums[b], 0.0)
        sobol_ref[g:g + 1] = part / total


def solve(cross, gram, block_group, scale):
    vmem = pl.BlockSpec(memory_space=pltpu.VMEM)
    cells = cross.shape[1]
    return pl.pallas_call(
        functools.partial(solve_kernel, scale),
        out_shape=(jax.ShapeDtypeStruct(cross.shape, F32), jax.ShapeDtypeStruct((GROUPS, cells), F32)),
        in_specs=[vmem, vmem, pl.BlockSpec(memory_space=pltpu.SMEM)],
        out_specs=(vmem, vmem),
        scratch_shapes=[pltpu.VMEM((4, 128, 512 + cells), F32), pltpu.VMEM((128, 128), F32)],
        compiler_params=pltpu.CompilerParams(vmem_limit_bytes=32 << 20),
        name="solve",
    )(cross, gram, block_group)


def exchange_kernel(coef_ref, out_ref, send_sem, recv_sem):
    samp, cell = lax.axis_index("samp"), lax.axis_index("cell")
    core = lax.rem(samp, 2)
    width = coef_ref.shape[1]
    rows = out_ref.shape[0]
    half = width // 2
    other = {"samp": samp + 1 - 2 * core, "cell": cell}
    distances = (2, 1, 3)
    peers = [lax.rem(cell + d, 4) for d in distances]
    barrier = pltpu.get_barrier_semaphore()
    for device in [other] + [{"samp": samp, "cell": v} for v in peers]:
        pl.semaphore_signal(barrier, inc=1, device_id=device, device_id_type=MESH)
    pl.semaphore_wait(barrier, 4)
    side = pl.ds(pl.multiple_of(core * half, 128), half)
    copies = []
    for n, v in enumerate(peers):
        copies.append(pltpu.make_async_remote_copy(
            src_ref=coef_ref.at[pl.ds(pl.multiple_of(v * rows, 8), rows), side],
            dst_ref=out_ref.at[:, pl.ds(pl.multiple_of(cell * width + core * half, 128), half)],
            send_sem=send_sem.at[n], recv_sem=recv_sem.at[n],
            device_id={"samp": samp, "cell": v}, device_id_type=MESH))
        copies[-1].start()
    out_ref[:, pl.ds(pl.multiple_of(cell * width, 128), width)] = coef_ref[pl.ds(pl.multiple_of(cell * rows, 8), rows), :]
    passed = []
    for n, d in ((1, 1), (2, 3), (0, 2)):
        source = lax.rem(cell + 4 - d, 4)
        copies[n].wait_recv()
        piece = out_ref.at[:, pl.ds(pl.multiple_of(source * width + core * half, 128), half)]
        passed.append(pltpu.make_async_remote_copy(
            src_ref=piece, dst_ref=piece, send_sem=send_sem.at[3 + n], recv_sem=recv_sem.at[3 + n],
            device_id=other, device_id_type=MESH))
        passed[-1].start()
    for copy in passed:
        copy.wait_recv()
    for copy in copies + passed:
        copy.wait_send()


def exchange(coef):
    vmem = pl.BlockSpec(memory_space=pltpu.VMEM)
    terms, cells = coef.shape
    return pl.pallas_call(
        exchange_kernel,
        out_shape=jax.ShapeDtypeStruct((terms // 4, cells * 4), F32),
        in_specs=[vmem],
        out_specs=vmem,
        scratch_shapes=[pltpu.SemaphoreType.DMA((6,)), pltpu.SemaphoreType.DMA((6,))],
        compiler_params=pltpu.CompilerParams(collective_id=1, has_side_effects=True),
        name="exchange",
    )(coef)


def on_device(points, yields, term_index, block_group):
    cross_local, gram_local = local_products(points, yields, term_index)
    cross, gram = sum_all(cross_local, gram_local)
    total_samples = points.shape[1] * lax.axis_size("samp")
    scaled, sobol = solve(cross, gram, block_group, float(total_samples) ** 0.5)
    return (exchange(scaled), sobol)


def solution(mesh):
    placed = (P(None, "samp"), P("samp", "cell"), P(), P())
    return jax.shard_map(
        on_device,
        mesh=mesh,
        in_specs=placed,
        out_specs=(P("cell", None), P(None, "cell")),
        check_vma=False,
    )
```

```python
import jax
import jax.numpy as jnp
from jax import lax
from jax.experimental import pallas as pl
from jax.experimental.pallas import tpu as pltpu
from jax.sharding import PartitionSpec as P

GROUPS = 8
TERMS = 512
HI = lax.Precision.HIGHEST
MESH = pl.DeviceIdType.MESH
F32 = jnp.float32
BF16 = jnp.bfloat16


def tile(start, size):
    return pl.ds(pl.multiple_of(start, 8), size)


def lanes(start, size):
    return pl.ds(pl.multiple_of(start, 128), size)


def basis(terms_ref, points_ref, psi_ref):
    params, samples = points_ref.shape
    width = 3 * params
    place = lax.broadcasted_iota(jnp.int32, (256, TERMS), 0)

    def pick(column):
        degree = column & 3
        target = (degree - 1) * params + (column >> 2)
        hit = (place == target) | (place == target + width) | (place == target + 2 * width)
        chosen = jnp.where(degree == 0, (place == 3 * width).astype(F32), hit.astype(F32))
        return chosen.T.astype(BF16)

    pick_a = pick(terms_ref[0:1, :])
    pick_b = pick(terms_ref[1:2, :])
    step = 512
    for start in range(0, samples, step):
        xs = points_ref[:, start:start + step]
        first = 1.7320508075688772 * xs
        second = 2.23606797749979 * (1.5 * xs * xs - 0.5)
        third = 2.6457513110645907 * (2.5 * xs * xs * xs - 1.5 * xs)
        degrees = jnp.concatenate([first, second, third], axis=0)
        high = degrees.astype(BF16).astype(F32)
        rest = degrees - high
        middle = rest.astype(BF16).astype(F32)
        low = rest - middle
        table = jnp.concatenate(
            [high, middle, low, jnp.ones((8, step), F32), jnp.zeros((256 - 3 * width - 8, step), F32)], axis=0
        ).astype(BF16)
        left = jnp.dot(pick_a, table, preferred_element_type=F32)
        right = jnp.dot(pick_b, table, preferred_element_type=F32)
        psi_ref[:, start:start + step] = (left * right).astype(BF16)


def gram_quarter(cell, psi_ref, gram_ref):
    low_half = cell < 2
    spots = (
        (0, 128, cell * 128, cell * 128),
        (128, 128, jnp.where(cell == 3, 0, cell * 128), jnp.minimum(cell + 1, 3) * 128),
        (256, 64, jnp.where(low_half, cell * 128, cell * 128 - 192), jnp.where(low_half, cell * 128 + 256, cell * 128)),
    )
    for place, rows, a, b in spots:
        one = psi_ref[pl.ds(pl.multiple_of(a, 64), rows), :]
        two = psi_ref[pl.ds(pl.multiple_of(b, 128), 128), :]
        gram_ref[place:place + rows, :] = lax.dot_general(one, two, (((1,), (1,)), ((), ())), preferred_element_type=F32)


def full(row):
    return jnp.broadcast_to(row, (8, 128))


def sweep_rows(rows, p, lane, sub):
    pivot = rows[p]
    at = 8 * p
    inside = (lane >= at) & (lane < at + 8)
    spread = [full(pivot[:, at + j:at + j + 1]) for j in range(8)]
    m = [[None] * 8 for _ in range(8)]
    for j in range(8):
        for i in range(j + 1):
            m[i][j] = full(spread[j][i:i + 1, :])
    for k in range(8):
        r = 1.0 / m[k][k]
        t = [None if j == k else m[min(j, k)][max(j, k)] * r for j in range(8)]
        old = [m[min(j, k)][max(j, k)] for j in range(8)]
        for j in range(8):
            for i in range(j + 1):
                if i != k and j != k:
                    m[i][j] = m[i][j] - old[i] * t[j]
        for j in range(8):
            if j != k:
                m[min(j, k)][max(j, k)] = t[j]
        m[k][k] = -r
    target = jnp.where(inside, jnp.where(lane - at == sub, 1.0, 0.0), -pivot)
    source = [full(target[i:i + 1, :]) for i in range(8)]
    wide = []
    for j in range(8):
        terms = [m[min(i, j)][max(i, j)] * source[i] for i in range(8)]
        wide.append(((terms[0] + terms[1]) + (terms[2] + terms[3])) + ((terms[4] + terms[5]) + (terms[6] + terms[7])))
    out = [None] * 16
    order = [(p + 1 + q) % 16 for q in range(15)]
    for q in order:
        terms = [full(rows[q][:, at + j:at + j + 1]) * wide[j] for j in range(8)]
        total = ((terms[0] + terms[1]) + (terms[2] + terms[3])) + ((terms[4] + terms[5]) + (terms[6] + terms[7]))
        out[q] = jnp.where(inside, 0.0, rows[q]) - total
    packed = wide[7]
    for j in range(7):
        packed = jnp.where(sub == j, wide[j], packed)
    out[p] = packed
    return out


def place_gram(gram_ref, a_ref):
    for b in range(4):
        a_ref[b, :, 128 * b:128 * b + 128] = gram_ref[b, 0:128]
    for b in range(3):
        a_ref[b, :, 128 * b + 128:128 * b + 256] = gram_ref[b, 128:256]
    a_ref[0, :, 384:512] = gram_ref[3, 128:256]
    for b in range(2):
        a_ref[b, 0:64, 128 * b + 256:128 * b + 384] = gram_ref[b, 256:320]
        a_ref[b, 64:128, 128 * b + 256:128 * b + 384] = gram_ref[b + 2, 256:320]


def fit_kernel(
    points_hbm, yields_hbm, terms_hbm, group_hbm, coef_out, share_out,
    points_ref, yields_ref, terms_ref, group_ref, psi_ref, cross_ref, gram_ref,
    got_gram, got_cross, half_gram, half_cross, y_gram, y_cross, part_gram, part_cross, z_gram, z_cross,
    all_gram, all_cross, whole_gram, whole_cross, a_ref, d_ref, x_ref,
    load_sem, core_s, core_r, y_s, y_r, zg_s, zg_r, zc_s, zc_r, bg_s, bg_r, bc_s, bc_r, yx_s, yx_r, yc_s, yc_r, x_s, x_r, f_s, f_r,
):
    samp, cell = lax.axis_index("samp"), lax.axis_index("cell")
    core = lax.rem(samp, 2)
    y = lax.rem(samp // 2, 4)
    z = samp // 8

    def at(zz, yy, cc, xx):
        return {"samp": (zz * 4 + yy) * 2 + cc, "cell": xx}

    def turn(v, d, n):
        return lax.rem(v + d, n)

    other = at(z, y, 1 - core, cell)
    far = (8, 7, 9, 6, 10, 5, 11, 4, 12, 3, 13, 2, 14, 1, 15)
    plane = [(dy, dx) for dy in (2, 1, 3, 0) for dx in (2, 1, 3, 0) if (dy, dx) != (0, 0)]
    barrier = pltpu.get_barrier_semaphore()
    greet = [at(turn(z, d, 16), y, core, cell) for d in far]
    greet += [at(z, turn(y, dy, 4), core, turn(cell, dx, 4)) for dy, dx in plane]
    greet += [other]
    for device in greet:
        pl.semaphore_signal(barrier, inc=1, device_id=device, device_id_type=MESH)

    loads = [
        pltpu.make_async_copy(terms_hbm, terms_ref, load_sem.at[0]),
        pltpu.make_async_copy(points_hbm, points_ref, load_sem.at[1]),
        pltpu.make_async_copy(yields_hbm, yields_ref, load_sem.at[2]),
        pltpu.make_async_copy(group_hbm, group_ref, load_sem.at[3]),
    ]
    for copy in loads:
        copy.start()
    loads[0].wait()
    loads[1].wait()
    basis(terms_ref, points_ref, psi_ref)
    gram_quarter(cell, psi_ref, gram_ref)
    loads[2].wait()
    cross_ref[...] = jnp.dot(psi_ref[...], yields_ref[...], preferred_element_type=F32)
    loads[3].wait()
    pl.semaphore_wait(barrier, len(greet))

    sent = []

    def remote(src, dst, s, r, device):
        return pltpu.make_async_remote_copy(
            src_ref=src, dst_ref=dst, send_sem=s, recv_sem=r, device_id=device, device_id_type=MESH)

    def go(*args):
        copy = remote(*args)
        copy.start()
        sent.append(copy)
        return copy

    def arrive(copies):
        for copy in copies:
            copy.wait_recv()

    core_g = go(gram_ref.at[tile((1 - core) * 160, 160)], got_gram, core_s.at[0], core_r.at[0], other)
    core_c = go(cross_ref.at[:, lanes((1 - core) * 128, 128)], got_cross, core_s.at[1], core_r.at[1], other)
    core_g.wait_recv()
    half_gram[...] = gram_ref[tile(core * 160, 160)] + got_gram[...]
    steps = (2, 1, 3)
    along_g = [
        go(half_gram.at[tile(turn(y, d, 4) * 40, 40)], y_gram.at[d - 1], y_s.at[d - 1], y_r.at[d - 1], at(z, turn(y, d, 4), core, cell))
        for d in steps]
    core_c.wait_recv()
    half_cross[...] = cross_ref[:, lanes(core * 128, 128)] + got_cross[...]
    along_c = [
        go(half_cross.at[tile(turn(y, d, 4) * 128, 128)], y_cross.at[d - 1], y_s.at[d + 2], y_r.at[d + 2], at(z, turn(y, d, 4), core, cell))
        for d in steps]

    arrive(along_g)
    part_gram[...] = (half_gram[tile(y * 40, 40)] + y_gram[0]) + (y_gram[1] + y_gram[2])
    to_owner = []
    for v in range(5):
        slot = lax.rem(z + 31 - v, 16)
        copy = remote(part_gram.at[8 * v:8 * v + 8], z_gram.at[jnp.minimum(slot, 14)], zg_s.at[v], zg_r.at[jnp.minimum(slot, 14)], at(v, y, core, cell))
        to_owner.append(copy)
        pl.when(z != v)(copy.start)
    arrive(along_c)
    part_cross[...] = (half_cross[tile(y * 128, 128)] + y_cross[0]) + (y_cross[1] + y_cross[2])
    z_c = [
        go(part_cross.at[tile(turn(z, d, 16) * 8, 8)], z_cross.at[d - 1], zc_s.at[d - 1], zc_r.at[d - 1], at(turn(z, d, 16), y, core, cell))
        for d in far]
    mine = tile(z * 8, 8)
    owned = tile(jnp.minimum(z, 4) * 8, 8)
    back_g = [
        remote(all_gram.at[owned], all_gram.at[owned], bg_s.at[d - 1], bg_r.at[jnp.minimum(z, 4)], at(turn(z, d, 16), y, core, cell))
        for d in far]

    def added(own, slots):
        values = [own] + [slots[d] for d in range(15)]
        while len(values) > 1:
            values = [values[i] + values[i + 1] for i in range(0, len(values), 2)]
        return values[0]

    @pl.when(z < 5)
    def _():
        for d in range(15):
            remote(part_gram.at[0:8], z_gram.at[d], zg_s.at[0], zg_r.at[d], other).wait_recv()
        all_gram[owned] = added(part_gram[owned], z_gram)
        for copy in back_g:
            copy.start()

    arrive(z_c)
    all_cross[mine] = added(part_cross[mine], z_cross)
    back_c = [
        go(all_cross.at[mine], all_cross.at[mine], bc_s.at[d - 1], bc_r.at[d - 1], at(turn(z, d, 16), y, core, cell))
        for d in far]

    for v in range(5):
        pl.when(z != v)(remote(part_gram.at[0:8], all_gram.at[8 * v:8 * v + 8], zg_s.at[0], bg_r.at[v], other).wait_recv)
    rows = tile(core * 160 + y * 40, 40)
    wide_g = [
        go(all_gram, whole_gram.at[cell, rows], yx_s.at[n], yx_r.at[n], at(z, turn(y, dy, 4), core, turn(cell, dx, 4)))
        for n, (dy, dx) in enumerate(plane)]
    whole_gram[cell, rows] = all_gram[...]
    arrive(back_c)
    spot = tile(y * 128, 128)
    side = lanes(core * 128, 128)
    wide_c = [
        go(all_cross, whole_cross.at[spot, side], yc_s.at[d - 1], yc_r.at[d - 1], at(z, turn(y, d, 4), core, cell))
        for d in steps]
    whole_cross[spot, side] = all_cross[...]
    arrive(wide_g)
    half = tile(core * 160, 160)
    pair_g = go(whole_gram.at[:, half], whole_gram.at[:, half], core_s.at[2], core_r.at[2], other)
    arrive(wide_c)
    pair_c = go(whole_cross.at[:, side], whole_cross.at[:, side], core_s.at[3], core_r.at[3], other)
    pair_g.wait_recv()

    place_gram(whole_gram, a_ref)
    d_ref[...] = a_ref[0, :, 0:128]
    lane = lax.broadcasted_iota(jnp.int32, (8, 128), 1)
    sub = lax.broadcasted_iota(jnp.int32, (8, 128), 0)
    cells = whole_cross.shape[1]
    end = 512 + cells

    def block(b, unused):
        held = [d_ref[8 * i:8 * i + 8, :] for i in range(16)]
        for p in range(16):
            held = sweep_rows(held, p, lane, sub)
        for i in range(16):
            d_ref[8 * i:8 * i + 8, :] = -held[i]
        for s in range(4):
            @pl.when(b == s)
            def _():
                if s == 0:
                    pair_c.wait_recv()
                    for i in range(4):
                        a_ref[i, :, 512:end] = whole_cross[128 * i:128 * i + 128]
                begin = 128 * s + 128
                w = jnp.dot(d_ref[...], a_ref[s, :, begin:end], precision=HI, preferred_element_type=F32)
                for i in range(s + 1, 4):
                    here = slice(128 * i, end)
                    a_ref[i, :, here] -= lax.dot_general(
                        a_ref[s, :, 128 * i:128 * i + 128], w[:, 128 * i - begin:], (((0,), (0,)), ((), ())), precision=HI, preferred_element_type=F32)
                a_ref[s, :, begin:end] = w
                if s < 3:
                    d_ref[...] = a_ref[s + 1, :, begin:begin + 128]
        return unused

    lax.fori_loop(0, 4, block, 0)
    column = cell * cells + core * 128
    found = [None] * 4
    handed = []
    for b in (3, 2, 1, 0):
        x = a_ref[b, :, 512:end]
        if b < 3:
            below = jnp.concatenate(found[b + 1:], axis=0)
            x = x - jnp.dot(a_ref[b, :, 128 * b + 128:512], below, precision=HI, preferred_element_type=F32)
        found[b] = x
        x_ref[b] = x
        copy = remote(
            x_ref.at[b, :, side], coef_out.at[:, lanes(column, 128)], x_s.at[b], x_r.at[cell], at(z, y, core, b))
        handed.append((b, copy))
        pl.when(cell != b)(copy.start)

    sums = []
    for b in range(4):
        sq = found[b] * found[b]
        if b == 0:
            sq = jnp.where(lax.broadcasted_iota(jnp.int32, sq.shape, 0) == 0, 0.0, sq)
        sums.append(jnp.sum(sq[0:64], axis=0, keepdims=True))
        sums.append(jnp.sum(sq[64:128], axis=0, keepdims=True))
    total = sums[0]
    for s in sums[1:]:
        total = total + s
    for g in range(GROUPS):
        part = jnp.zeros_like(total)
        for b in range(8):
            part = part + jnp.where(group_ref[b] == g, sums[b], 0.0)
        share_out[g:g + 1] = part / total
    coef_out[:, lanes(cell * cells, cells)] = x_ref[cell]

    passed = []
    for d in (1, 3, 2):
        source = turn(cell, d, 4)
        piece = coef_out.at[:, lanes(source * cells + core * 128, 128)]
        remote(x_ref.at[0, :, side], piece, x_s.at[0], x_r.at[source], other).wait_recv()
        passed.append(go(piece, piece, f_s.at[d - 1], f_r.at[d - 1], other))
    arrive(passed)
    for copy in sent:
        copy.wait_send()
    for v in range(5):
        pl.when(z != v)(to_owner[v].wait_send)
    for b, copy in handed:
        pl.when(cell != b)(copy.wait_send)

    @pl.when(z < 5)
    def _():
        for copy in back_g:
            copy.wait_send()


def fit(points, yields, term_index, block_group):
    hbm = pl.BlockSpec(memory_space=pltpu.HBM)
    vmem = pl.BlockSpec(memory_space=pltpu.VMEM)
    params, samples = points.shape
    cells = yields.shape[1]
    dma = pltpu.SemaphoreType.DMA

    def f32(*shape):
        return pltpu.VMEM(shape, F32)

    return pl.pallas_call(
        fit_kernel,
        out_shape=(jax.ShapeDtypeStruct((TERMS // 4, cells * 4), F32), jax.ShapeDtypeStruct((GROUPS, cells), F32)),
        in_specs=[hbm] * 4,
        out_specs=(vmem, vmem),
        scratch_shapes=[
            f32(params, samples), pltpu.VMEM((samples, cells), BF16), pltpu.VMEM((2, TERMS), jnp.int32), pltpu.SMEM((8,), jnp.int32),
            pltpu.VMEM((TERMS, samples), BF16), f32(TERMS, cells), f32(320, 128),
            f32(160, 128), f32(512, 128), f32(160, 128), f32(512, 128), f32(3, 40, 128), f32(3, 128, 128), f32(40, 128), f32(128, 128),
            f32(15, 8, 128), f32(15, 8, 128), f32(40, 128), f32(128, 128), f32(4, 320, 128), f32(TERMS, cells),
            f32(4, 128, 512 + cells), f32(128, 128), f32(4, 128, cells),
            dma((4,)), dma((4,)), dma((4,)), dma((6,)), dma((6,)), dma((5,)), dma((15,)), dma((15,)), dma((15,)), dma((15,)), dma((5,)),
            dma((15,)), dma((15,)), dma((15,)), dma((15,)), dma((3,)), dma((3,)), dma((4,)), dma((4,)), dma((3,)), dma((3,)),
        ],
        compiler_params=pltpu.CompilerParams(collective_id=0, has_side_effects=True, vmem_limit_bytes=63 << 20),
        name="fit",
    )(points, yields, term_index.T, block_group)


def on_device(points, yields, term_index, block_group):
    coef, sobol = fit(points, yields, term_index, block_group)
    total_samples = points.shape[1] * lax.axis_size("samp")
    return (coef * jnp.sqrt(jnp.float32(total_samples)), sobol)


def solution(mesh):
    placed = (P(None, "samp"), P("samp", "cell"), P(), P())
    return jax.shard_map(
        on_device,
        mesh=mesh,
        in_specs=placed,
        out_specs=(P("cell", None), P(None, "cell")),
        check_vma=False,
    )
```

```python
import functools

import jax
import jax.numpy as jnp
from jax import lax
from jax.experimental import pallas as pl
from jax.experimental.pallas import tpu as pltpu
from jax.sharding import PartitionSpec as P

GROUPS = 8
TERMS = 512
MESH = pl.DeviceIdType.MESH
F32 = jnp.float32
BF16 = jnp.bfloat16


def tile(start, size):
    return pl.ds(pl.multiple_of(start, 8), size)


def lanes(start, size):
    return pl.ds(pl.multiple_of(start, 128), size)


def basis(terms_ref, points_ref, psi_ref):
    params, samples = points_ref.shape
    width = 3 * params
    place = lax.broadcasted_iota(jnp.int32, (256, TERMS), 0)
    order = [128 * quarter + 32 * block for block in range(4) for quarter in range(4)]

    def pick(column):
        degree = column & 3
        target = (degree - 1) * params + (column >> 2)
        hit = (place == target) | (place == target + width) | (place == target + 2 * width)
        chosen = jnp.where(degree == 0, (place == 3 * width).astype(F32), hit.astype(F32))
        straight = chosen.T
        return jnp.concatenate([straight[start:start + 32] for start in order], axis=0).astype(BF16)

    pick_a = pick(terms_ref[0:1, :])
    pick_b = pick(terms_ref[1:2, :])
    step = 512
    for start in range(0, samples, step):
        xs = points_ref[:, start:start + step]
        first = 1.7320508075688772 * xs
        second = 2.23606797749979 * (1.5 * xs * xs - 0.5)
        third = 2.6457513110645907 * (2.5 * xs * xs * xs - 1.5 * xs)
        degrees = jnp.concatenate([first, second, third], axis=0)
        high = degrees.astype(BF16).astype(F32)
        rest = degrees - high
        middle = rest.astype(BF16).astype(F32)
        low = rest - middle
        table = jnp.concatenate(
            [high, middle, low, jnp.ones((8, step), F32), jnp.zeros((256 - 3 * width - 8, step), F32)], axis=0
        ).astype(BF16)
        left = jnp.dot(pick_a, table, preferred_element_type=F32)
        right = jnp.dot(pick_b, table, preferred_element_type=F32)
        psi_ref[:, start:start + step] = (left * right).astype(BF16)


def gram_quarter(cell, psi_ref, gram_ref):
    low_half = cell < 2
    spots = (
        (0, 128, cell * 128, cell * 128),
        (128, 128, jnp.where(cell == 3, 0, cell * 128), jnp.minimum(cell + 1, 3) * 128),
        (256, 64, jnp.where(low_half, cell * 128, cell * 128 - 192), jnp.where(low_half, cell * 128 + 256, cell * 128)),
    )
    for place, rows, a, b in spots:
        one = psi_ref[pl.ds(pl.multiple_of(a, 64), rows), :]
        two = psi_ref[pl.ds(pl.multiple_of(b, 128), 128), :]
        gram_ref[place:place + rows, :] = lax.dot_general(one, two, (((1,), (1,)), ((), ())), preferred_element_type=F32)


def full(row):
    return jnp.broadcast_to(row, (8, 128))


def tree(terms):
    terms = list(terms)
    while len(terms) > 1:
        terms = [terms[i] + terms[i + 1] for i in range(0, len(terms), 2)]
    return terms[0]


def parts(v):
    a = v.astype(BF16)
    rest = v - a.astype(F32)
    b = rest.astype(BF16)
    return a, b, (rest - b.astype(F32)).astype(BF16)


def as_left(v, axis):
    a, b, c = parts(v)
    return jnp.concatenate([a, a, b, b, a, c], axis=axis)


def as_right(v):
    a, b, c = parts(v)
    return jnp.concatenate([a, b, a, b, c, a], axis=0)


def mul(left, right, axis):
    return lax.dot_general(left, right, (((axis,), (0,)), ((), ())), preferred_element_type=F32)


def sweep_rows(rows, p, lane, sub, spill):
    pivot = rows[p]
    at = 8 * p
    inside = (lane >= at) & (lane < at + 8)
    target = jnp.where(inside, jnp.where(lane - at == sub, 1.0, 0.0), -pivot)
    base = 9 * (p % 2)
    for j in range(8):
        spill[base + j] = full(pivot[:, at + j:at + j + 1])
    spill[base + 8] = target

    def row(k, i):
        return spill[base + k, pl.ds(i, 8, stride=0), :]

    m = [[None] * 8 for _ in range(8)]
    for j in range(8):
        for i in range(j + 1):
            m[i][j] = row(j, i)
    for k in range(8):
        r = 1.0 / m[k][k]
        old = [m[min(j, k)][max(j, k)] for j in range(8)]
        t = [None if j == k else old[j] * r for j in range(8)]
        for j in range(8):
            for i in range(j + 1):
                if i != k and j != k:
                    m[i][j] = m[i][j] - old[i] * t[j]
        for j in range(8):
            if j != k:
                m[min(j, k)][max(j, k)] = t[j]
        m[k][k] = -r
    source = [row(8, i) for i in range(8)]
    wide = [tree([m[min(i, j)][max(i, j)] * source[i] for i in range(8)]) for j in range(8)]
    out = list(rows)
    near = [q for q in (p + 1, p + 2) if q < 16]
    for q in near:
        out[q] = jnp.where(inside, 0.0, rows[q]) - tree([full(rows[q][:, at + j:at + j + 1]) * wide[j] for j in range(8)])
    packed = wide[7]
    for j in range(7):
        packed = jnp.where(sub == j, wide[j], packed)
    u = [v.astype(F32) for v in parts(pivot)]
    w = [v.astype(F32) for v in parts(packed)]
    left = jnp.concatenate([u[0], u[0], u[1], u[1], u[0], u[2]], axis=0).astype(BF16)
    right = jnp.concatenate([w[0], w[1], w[0], w[1], w[2], w[0]], axis=0).astype(BF16)
    change = mul(left, right, 0)
    for q in range(16):
        if q != p and q not in near:
            out[q] = jnp.where(inside, 0.0, rows[q]) - change[8 * q:8 * q + 8]
    out[p] = packed
    return out


def invert(block, spill):
    lane = lax.broadcasted_iota(jnp.int32, (8, 128), 1)
    sub = lax.broadcasted_iota(jnp.int32, (8, 128), 0)
    rows = [block[8 * i:8 * i + 8] for i in range(16)]
    for p in range(16):
        rows = sweep_rows(rows, p, lane, sub, spill)
    return -jnp.concatenate(rows, axis=0)


def eliminate(a_ref, spill, late):
    end = a_ref.shape[2]
    diag = a_ref[0, :, 0:128]
    for b in range(4):
        inverse = invert(diag, spill)
        if b == 0:
            late()
        p = as_left(inverse, 1)
        begin = 128 * b + 128
        if b < 3:
            s1 = a_ref[b, :, begin:begin + 128]
            w1 = mul(p, as_right(s1), 1)
            diag = a_ref[b + 1, :, begin:begin + 128] - mul(as_left(s1, 0), as_right(w1), 0)
            a_ref[b, :, begin:begin + 128] = w1
        cut = min(begin + 128, 512)
        s2 = a_ref[b, :, cut:end]
        w2 = mul(p, as_right(s2), 1)
        a_ref[b, :, cut:end] = w2
        if b < 3:
            right = as_right(w2)
            a_ref[b + 1, :, cut:end] -= mul(as_left(s1, 0), right, 0)
            for i in range(b + 2, 4):
                left = as_left(s2[:, 128 * i - cut:128 * i - cut + 128], 0)
                a_ref[i, :, 128 * i:end] -= mul(left, right[:, 128 * i - cut:], 0)
    for b in (3, 2, 1, 0):
        x = a_ref[b, :, 512:end]
        yield b, x
        right = as_right(x)
        for i in range(b - 1, -1, -1):
            a_ref[i, :, 512:end] -= mul(as_left(a_ref[i, :, 128 * b:128 * b + 128], 1), right, 1)


def place_gram(gram_ref, a_ref):
    for b in range(4):
        a_ref[b, :, 128 * b:128 * b + 128] = gram_ref[b, 0:128]
    for b in range(3):
        a_ref[b, :, 128 * b + 128:128 * b + 256] = gram_ref[b, 128:256]
    a_ref[0, :, 384:512] = gram_ref[3, 128:256]
    for b in range(2):
        a_ref[b, 0:64, 128 * b + 256:128 * b + 384] = gram_ref[b, 256:320]
        a_ref[b, 64:128, 128 * b + 256:128 * b + 384] = gram_ref[b + 2, 256:320]


def fit_kernel(
    points_hbm, yields_hbm, terms_hbm, group_hbm, coef_out, share_out,
    points_ref, yields_ref, terms_ref, group_ref, psi_ref, cross_ref, gram_ref,
    got_gram, got_cross, half_gram, half_cross, y_gram, y_cross, part_gram, part_cross, z_gram, z_cross,
    all_gram, all_cross, whole_gram, whole_cross, a_ref, spill_ref, x_ref,
    load_sem, core_s, core_r, y_s, y_r, zg_s, zg_r, zc_s, zc_r, bg_s, bg_r, bc_s, bc_r, yx_s, yx_r, yc_s, yc_r, x_s, x_r, f_s, f_r,
):
    samp, cell = lax.axis_index("samp"), lax.axis_index("cell")
    core = lax.rem(samp, 2)
    y = lax.rem(samp // 2, 4)
    z = samp // 8

    def at(zz, yy, cc, xx):
        return {"samp": (zz * 4 + yy) * 2 + cc, "cell": xx}

    def turn(v, d, n):
        return lax.rem(v + d, n)

    other = at(z, y, 1 - core, cell)
    far = (8, 7, 9, 6, 10, 5, 11, 4, 12, 3, 13, 2, 14, 1, 15)
    plane = [(dy, dx) for dy in (2, 1, 3, 0) for dx in (2, 1, 3, 0) if (dy, dx) != (0, 0)]
    barrier = pltpu.get_barrier_semaphore()
    greet = [at(turn(z, d, 16), y, core, cell) for d in far]
    greet += [at(z, turn(y, dy, 4), core, turn(cell, dx, 4)) for dy, dx in plane]
    greet += [other]
    for device in greet:
        pl.semaphore_signal(barrier, inc=1, device_id=device, device_id_type=MESH)

    loads = [
        pltpu.make_async_copy(terms_hbm, terms_ref, load_sem.at[0]),
        pltpu.make_async_copy(points_hbm, points_ref, load_sem.at[1]),
        pltpu.make_async_copy(yields_hbm, yields_ref, load_sem.at[2]),
        pltpu.make_async_copy(group_hbm, group_ref, load_sem.at[3]),
    ]
    for copy in loads:
        copy.start()
    loads[0].wait()
    loads[1].wait()
    basis(terms_ref, points_ref, psi_ref)
    gram_quarter(cell, psi_ref, gram_ref)
    loads[2].wait()
    cross_ref[...] = jnp.dot(psi_ref[...], yields_ref[...], preferred_element_type=F32)
    loads[3].wait()
    pl.semaphore_wait(barrier, len(greet))

    sent = []

    def remote(src, dst, s, r, device):
        return pltpu.make_async_remote_copy(
            src_ref=src, dst_ref=dst, send_sem=s, recv_sem=r, device_id=device, device_id_type=MESH)

    def go(*args):
        copy = remote(*args)
        copy.start()
        sent.append(copy)
        return copy

    def arrive(copies):
        for copy in copies:
            copy.wait_recv()

    core_g = go(gram_ref.at[tile((1 - core) * 160, 160)], got_gram, core_s.at[0], core_r.at[0], other)
    core_c = go(cross_ref.at[:, lanes((1 - core) * 128, 128)], got_cross, core_s.at[1], core_r.at[1], other)
    core_g.wait_recv()
    half_gram[...] = gram_ref[tile(core * 160, 160)] + got_gram[...]
    steps = (2, 1, 3)
    along_g = [
        go(half_gram.at[tile(turn(y, d, 4) * 40, 40)], y_gram.at[d - 1], y_s.at[d - 1], y_r.at[d - 1], at(z, turn(y, d, 4), core, cell))
        for d in steps]
    core_c.wait_recv()
    half_cross[...] = cross_ref[:, lanes(core * 128, 128)] + got_cross[...]
    along_c = [
        go(half_cross.at[tile(turn(y, d, 4) * 128, 128)], y_cross.at[d - 1], y_s.at[d + 2], y_r.at[d + 2], at(z, turn(y, d, 4), core, cell))
        for d in steps]

    arrive(along_g)
    part_gram[...] = (half_gram[tile(y * 40, 40)] + y_gram[0]) + (y_gram[1] + y_gram[2])
    to_owner = []
    for v in range(5):
        slot = lax.rem(z + 31 - v, 16)
        copy = remote(part_gram.at[8 * v:8 * v + 8], z_gram.at[jnp.minimum(slot, 14)], zg_s.at[v], zg_r.at[jnp.minimum(slot, 14)], at(v, y, core, cell))
        to_owner.append(copy)
        pl.when(z != v)(copy.start)
    arrive(along_c)
    part_cross[...] = (half_cross[tile(y * 128, 128)] + y_cross[0]) + (y_cross[1] + y_cross[2])
    z_c = [
        go(part_cross.at[tile(turn(z, d, 16) * 8, 8)], z_cross.at[d - 1], zc_s.at[d - 1], zc_r.at[d - 1], at(turn(z, d, 16), y, core, cell))
        for d in far]
    mine = tile(z * 8, 8)
    owned = tile(jnp.minimum(z, 4) * 8, 8)
    back_g = [
        remote(all_gram.at[owned], all_gram.at[owned], bg_s.at[d - 1], bg_r.at[jnp.minimum(z, 4)], at(turn(z, d, 16), y, core, cell))
        for d in far]

    def added(own, slots):
        return tree([own] + [slots[d] for d in range(15)])

    @pl.when(z < 5)
    def _():
        for d in range(15):
            remote(part_gram.at[0:8], z_gram.at[d], zg_s.at[0], zg_r.at[d], other).wait_recv()
        all_gram[owned] = added(part_gram[owned], z_gram)
        for copy in back_g:
            copy.start()

    arrive(z_c)
    all_cross[mine] = added(part_cross[mine], z_cross)
    back_c = [
        go(all_cross.at[mine], all_cross.at[mine], bc_s.at[d - 1], bc_r.at[d - 1], at(turn(z, d, 16), y, core, cell))
        for d in far]

    for v in range(5):
        pl.when(z != v)(remote(part_gram.at[0:8], all_gram.at[8 * v:8 * v + 8], zg_s.at[0], bg_r.at[v], other).wait_recv)
    rows = tile(core * 160 + y * 40, 40)
    wide_g = [
        go(all_gram, whole_gram.at[cell, rows], yx_s.at[n], yx_r.at[n], at(z, turn(y, dy, 4), core, turn(cell, dx, 4)))
        for n, (dy, dx) in enumerate(plane)]
    whole_gram[cell, rows] = all_gram[...]
    arrive(back_c)
    spot = tile(y * 128, 128)
    side = lanes(core * 128, 128)
    wide_c = [
        go(all_cross, whole_cross.at[spot, side], yc_s.at[d - 1], yc_r.at[d - 1], at(z, turn(y, d, 4), core, cell))
        for d in steps]
    whole_cross[spot, side] = all_cross[...]
    arrive(wide_g)
    half = tile(core * 160, 160)
    pair_g = go(whole_gram.at[:, half], whole_gram.at[:, half], core_s.at[2], core_r.at[2], other)
    arrive(wide_c)
    pair_c = go(whole_cross.at[:, side], whole_cross.at[:, side], core_s.at[3], core_r.at[3], other)
    pair_g.wait_recv()

    place_gram(whole_gram, a_ref)
    cells = whole_cross.shape[1]

    def late():
        pair_c.wait_recv()
        for i in range(4):
            a_ref[i, :, 512:512 + cells] = whole_cross[128 * i:128 * i + 128]

    column = cell * cells + core * 128
    own = lanes(cell * cells, cells)
    found = [None] * 4
    handed = []
    for b, x in eliminate(a_ref, spill_ref, late):
        found[b] = x
        x_ref[b] = x
        for v in range(4):
            copy = remote(
                x_ref.at[b, 32 * v:32 * v + 32, side], coef_out.at[32 * b:32 * b + 32, lanes(column, 128)],
                x_s.at[4 * b + v], x_r.at[4 * b + cell], at(z, y, core, v))
            handed.append((v, copy))
            pl.when(cell != v)(copy.start)
        coef_out[32 * b:32 * b + 32, own] = x_ref[b, tile(cell * 32, 32), :]

    sums = []
    for quarter in range(4):
        for low in (0, 2):
            value = None
            for b in (low, low + 1):
                sq = found[b][32 * quarter:32 * quarter + 32] * found[b][32 * quarter:32 * quarter + 32]
                if quarter == 0 and b == 0:
                    sq = jnp.where(lax.broadcasted_iota(jnp.int32, sq.shape, 0) == 0, 0.0, sq)
                value = sq if value is None else value + sq
            sums.append(jnp.sum(value, axis=0, keepdims=True))
    total = sums[0]
    for s in sums[1:]:
        total = total + s
    for g in range(GROUPS):
        part = jnp.zeros_like(total)
        for b in range(8):
            part = part + jnp.where(group_ref[b] == g, sums[b], 0.0)
        share_out[g:g + 1] = part / total

    passed = []
    for n, blocks in enumerate(((3, 2, 1), (0,))):
        piece_rows = slice(32 * min(blocks), 32 * max(blocks) + 32)
        for d in (1, 3, 2):
            source = turn(cell, d, 4)
            place = lanes(source * cells + core * 128, 128)
            for b in blocks:
                remote(x_ref.at[0, 0:32, side], coef_out.at[32 * b:32 * b + 32, place], x_s.at[0], x_r.at[4 * b + source], other).wait_recv()
            piece = coef_out.at[piece_rows, place]
            passed.append(go(piece, piece, f_s.at[3 * n + d - 1], f_r.at[3 * n + d - 1], other))
    arrive(passed)
    for copy in sent:
        copy.wait_send()
    for v in range(5):
        pl.when(z != v)(to_owner[v].wait_send)
    for v, copy in handed:
        pl.when(cell != v)(copy.wait_send)

    @pl.when(z < 5)
    def _():
        for copy in back_g:
            copy.wait_send()


def fit(points, yields, term_index, block_group):
    hbm = pl.BlockSpec(memory_space=pltpu.HBM)
    vmem = pl.BlockSpec(memory_space=pltpu.VMEM)
    params, samples = points.shape
    cells = yields.shape[1]
    dma = pltpu.SemaphoreType.DMA

    def f32(*shape):
        return pltpu.VMEM(shape, F32)

    points, yields, terms, block_group = (
        pltpu.with_memory_space_constraint(v, pltpu.HBM) for v in (points, yields, term_index.T, block_group))
    return pl.pallas_call(
        fit_kernel,
        out_shape=(jax.ShapeDtypeStruct((TERMS // 4, cells * 4), F32), jax.ShapeDtypeStruct((GROUPS, cells), F32)),
        in_specs=[hbm] * 4,
        out_specs=(vmem, vmem),
        scratch_shapes=[
            f32(params, samples), pltpu.VMEM((samples, cells), BF16), pltpu.VMEM((2, TERMS), jnp.int32), pltpu.SMEM((8,), jnp.int32),
            pltpu.VMEM((TERMS, samples), BF16), f32(TERMS, cells), f32(320, 128),
            f32(160, 128), f32(512, 128), f32(160, 128), f32(512, 128), f32(3, 40, 128), f32(3, 128, 128), f32(40, 128), f32(128, 128),
            f32(15, 8, 128), f32(15, 8, 128), f32(40, 128), f32(128, 128), f32(4, 320, 128), f32(TERMS, cells),
            f32(4, 128, 512 + cells), f32(18, 8, 128), f32(4, 128, cells),
            dma((4,)), dma((4,)), dma((4,)), dma((6,)), dma((6,)), dma((5,)), dma((15,)), dma((15,)), dma((15,)), dma((15,)), dma((5,)),
            dma((15,)), dma((15,)), dma((15,)), dma((15,)), dma((3,)), dma((3,)), dma((16,)), dma((16,)), dma((6,)), dma((6,)),
        ],
        compiler_params=pltpu.CompilerParams(collective_id=0, has_side_effects=True, vmem_limit_bytes=48 << 20),
        name="fit",
    )(points, yields, terms, block_group)


def finish_kernel(scale, coef_ref, share_ref, coef_hbm, share_hbm, scaled_ref, sem):
    copies = [pltpu.make_async_copy(share_ref, share_hbm, sem.at[4])]
    copies[0].start()
    for n in range(4):
        rows = slice(32 * n, 32 * n + 32)
        scaled_ref[rows] = coef_ref[rows] * scale
        copies.append(pltpu.make_async_copy(scaled_ref.at[rows], coef_hbm.at[rows], sem.at[n]))
        copies[-1].start()
    for copy in copies:
        copy.wait()


def finish(coef, share, scale):
    hbm = pl.BlockSpec(memory_space=pltpu.HBM)
    vmem = pl.BlockSpec(memory_space=pltpu.VMEM)
    return pl.pallas_call(
        functools.partial(finish_kernel, scale),
        out_shape=(jax.ShapeDtypeStruct(coef.shape, F32), jax.ShapeDtypeStruct(share.shape, F32)),
        in_specs=[vmem, vmem],
        out_specs=(hbm, hbm),
        scratch_shapes=[pltpu.VMEM(coef.shape, F32), pltpu.SemaphoreType.DMA((5,))],
        compiler_params=pltpu.CompilerParams(vmem_limit_bytes=4 << 20),
        name="finish",
    )(coef, share)


def on_device(points, yields, term_index, block_group):
    coef, sobol = fit(points, yields, term_index, block_group)
    return finish(coef, sobol, float(points.shape[1] * lax.axis_size("samp")) ** 0.5)


def solution(mesh):
    placed = (P(None, "samp"), P("samp", "cell"), P(), P())
    return jax.shard_map(
        on_device,
        mesh=mesh,
        in_specs=placed,
        out_specs=(P("cell", None), P(None, "cell")),
        check_vma=False,
    )
```

```python
import functools

import jax
import jax.numpy as jnp
from jax import lax
from jax.experimental import pallas as pl
from jax.experimental.pallas import tpu as pltpu
from jax.sharding import PartitionSpec as P

GROUPS = 8
TERMS = 512
MESH = pl.DeviceIdType.MESH
F32 = jnp.float32
BF16 = jnp.bfloat16


def tile(start, size):
    return pl.ds(pl.multiple_of(start, 8), size)


def lanes(start, size):
    return pl.ds(pl.multiple_of(start, 128), size)


def basis(terms_ref, points_ref, psi_ref):
    params, samples = points_ref.shape
    width = 3 * params
    place = lax.broadcasted_iota(jnp.int32, (256, TERMS), 0)
    order = [128 * quarter + 32 * block for block in range(4) for quarter in range(4)]

    def pick(column):
        degree = column & 3
        target = (degree - 1) * params + (column >> 2)
        hit = (place == target) | (place == target + width) | (place == target + 2 * width)
        chosen = jnp.where(degree == 0, (place == 3 * width).astype(F32), hit.astype(F32))
        straight = chosen.T
        return jnp.concatenate([straight[start:start + 32] for start in order], axis=0).astype(BF16)

    pick_a = pick(terms_ref[0:1, :])
    pick_b = pick(terms_ref[1:2, :])
    step = 512
    for start in range(0, samples, step):
        xs = points_ref[:, start:start + step]
        first = 1.7320508075688772 * xs
        second = 2.23606797749979 * (1.5 * xs * xs - 0.5)
        third = 2.6457513110645907 * (2.5 * xs * xs * xs - 1.5 * xs)
        degrees = jnp.concatenate([first, second, third], axis=0)
        high = degrees.astype(BF16).astype(F32)
        rest = degrees - high
        middle = rest.astype(BF16).astype(F32)
        low = rest - middle
        table = jnp.concatenate(
            [high, middle, low, jnp.ones((8, step), F32), jnp.zeros((256 - 3 * width - 8, step), F32)], axis=0
        ).astype(BF16)
        left = jnp.dot(pick_a, table, preferred_element_type=F32)
        right = jnp.dot(pick_b, table, preferred_element_type=F32)
        psi_ref[:, start:start + step] = (left * right).astype(BF16)


def gram_quarter(cell, psi_ref, gram_ref, corner_ref):
    corner_ref[...] = lax.dot_general(
        psi_ref[pl.ds(pl.multiple_of(cell * 32, 32), 32), :], psi_ref[0:128, :], (((1,), (1,)), ((), ())), preferred_element_type=F32)
    low_half = cell < 2
    spots = (
        (0, 128, cell * 128, cell * 128),
        (128, 128, jnp.where(cell == 3, 0, cell * 128), jnp.minimum(cell + 1, 3) * 128),
        (256, 64, jnp.where(low_half, cell * 128, cell * 128 - 192), jnp.where(low_half, cell * 128 + 256, cell * 128)),
    )
    for place, rows, a, b in spots:
        one = psi_ref[pl.ds(pl.multiple_of(a, 64), rows), :]
        two = psi_ref[pl.ds(pl.multiple_of(b, 128), 128), :]
        gram_ref[place:place + rows, :] = lax.dot_general(one, two, (((1,), (1,)), ((), ())), preferred_element_type=F32)


def full(row):
    return jnp.broadcast_to(row, (8, 128))


def tree(terms):
    terms = list(terms)
    while len(terms) > 1:
        terms = [terms[i] + terms[i + 1] for i in range(0, len(terms), 2)]
    return terms[0]


def parts(v):
    a = v.astype(BF16)
    rest = v - a.astype(F32)
    b = rest.astype(BF16)
    return a, b, (rest - b.astype(F32)).astype(BF16)


def as_left(v, axis):
    a, b, c = parts(v)
    return jnp.concatenate([a, a, b, b, a, c], axis=axis)


def as_right(v):
    a, b, c = parts(v)
    return jnp.concatenate([a, b, a, b, c, a], axis=0)


def mul(left, right, axis):
    return lax.dot_general(left, right, (((axis,), (0,)), ((), ())), preferred_element_type=F32)


def sweep_rows(rows, p, lane, sub, spill):
    pivot = rows[p]
    at = 8 * p
    inside = (lane >= at) & (lane < at + 8)
    target = jnp.where(inside, jnp.where(lane - at == sub, 1.0, 0.0), -pivot)
    base = 9 * (p % 2)
    for j in range(8):
        spill[base + j] = full(pivot[:, at + j:at + j + 1])
    spill[base + 8] = target

    def row(k, i):
        return spill[base + k, pl.ds(i, 8, stride=0), :]

    m = [[None] * 8 for _ in range(8)]
    for j in range(8):
        for i in range(j + 1):
            m[i][j] = row(j, i)
    for k in range(8):
        r = 1.0 / m[k][k]
        old = [m[min(j, k)][max(j, k)] for j in range(8)]
        t = [None if j == k else old[j] * r for j in range(8)]
        for j in range(8):
            for i in range(j + 1):
                if i != k and j != k:
                    m[i][j] = m[i][j] - old[i] * t[j]
        for j in range(8):
            if j != k:
                m[min(j, k)][max(j, k)] = t[j]
        m[k][k] = -r
    source = [row(8, i) for i in range(8)]
    wide = [tree([m[min(i, j)][max(i, j)] * source[i] for i in range(8)]) for j in range(8)]
    out = list(rows)
    near = [q for q in (p + 1, p + 2) if q < 16]
    for q in near:
        out[q] = jnp.where(inside, 0.0, rows[q]) - tree([full(rows[q][:, at + j:at + j + 1]) * wide[j] for j in range(8)])
    packed = wide[7]
    for j in range(7):
        packed = jnp.where(sub == j, wide[j], packed)
    u = [v.astype(F32) for v in parts(pivot)]
    w = [v.astype(F32) for v in parts(packed)]
    left = jnp.concatenate([u[0], u[0], u[1], u[1], u[0], u[2]], axis=0).astype(BF16)
    right = jnp.concatenate([w[0], w[1], w[0], w[1], w[2], w[0]], axis=0).astype(BF16)
    change = mul(left, right, 0)
    for q in range(16):
        if q != p and q not in near:
            out[q] = jnp.where(inside, 0.0, rows[q]) - change[8 * q:8 * q + 8]
    out[p] = packed
    return out


def invert(block, spill, between):
    lane = lax.broadcasted_iota(jnp.int32, (8, 128), 1)
    sub = lax.broadcasted_iota(jnp.int32, (8, 128), 0)
    rows = [block[8 * i:8 * i + 8] for i in range(16)]
    for p in range(16):
        if p in between:
            between[p]()
        rows = sweep_rows(rows, p, lane, sub, spill)
    return -jnp.concatenate(rows, axis=0)


def eliminate(corner, a_ref, spill, between, after):
    end = a_ref.shape[2]
    diag = corner
    kept = []

    def forward(b):
        right = as_right(a_ref[b, :, 512:end])
        for i in range(b + 1, 4):
            a_ref[i, :, 512:end] -= mul(as_left(a_ref[b, :, 128 * i:128 * i + 128], 0), right, 0)
        a_ref[b, :, 512:end] = mul(kept[b], right, 1)

    for b in range(4):
        inverse = invert(diag, spill, between.get(b, {}))
        after.get(b, lambda: None)()
        p = as_left(inverse, 1)
        kept.append(p)
        begin = 128 * b + 128
        if b < 3:
            s1 = a_ref[b, :, begin:begin + 128]
            w1 = mul(p, as_right(s1), 1)
            diag = a_ref[b + 1, :, begin:begin + 128] - mul(as_left(s1, 0), as_right(w1), 0)
            a_ref[b, :, begin:begin + 128] = w1
        if b < 2:
            cut = begin + 128
            s2 = a_ref[b, :, cut:512]
            w2 = mul(p, as_right(s2), 1)
            a_ref[b, :, cut:512] = w2
            right = as_right(w2)
            a_ref[b + 1, :, cut:512] -= mul(as_left(s1, 0), right, 0)
            for i in range(b + 2, 4):
                left = as_left(s2[:, 128 * i - cut:128 * i - cut + 128], 0)
                a_ref[i, :, 128 * i:512] -= mul(left, right[:, 128 * i - cut:], 0)
        if b > 0:
            forward(b - 1)
    forward(3)
    for b in (3, 2, 1, 0):
        x = a_ref[b, :, 512:end]
        yield b, x
        right = as_right(x)
        for i in range(b - 1, -1, -1):
            a_ref[i, :, 512:end] -= mul(as_left(a_ref[i, :, 128 * b:128 * b + 128], 1), right, 1)


def place_gram(gram_ref, a_ref):
    for b in range(1, 4):
        a_ref[b, :, 128 * b:128 * b + 128] = gram_ref[b, 0:128]
    for b in range(3):
        a_ref[b, :, 128 * b + 128:128 * b + 256] = gram_ref[b, 128:256]
    a_ref[0, :, 384:512] = gram_ref[3, 128:256]
    for b in range(2):
        a_ref[b, 0:64, 128 * b + 256:128 * b + 384] = gram_ref[b, 256:320]
        a_ref[b, 64:128, 128 * b + 256:128 * b + 384] = gram_ref[b + 2, 256:320]


def fit_kernel(
    points_hbm, yields_hbm, terms_hbm, group_hbm, coef_out, share_out,
    points_ref, yields_ref, terms_ref, group_ref, psi_ref, cross_ref, gram_ref, corner_ref, near_ref, line_ref, first_ref,
    y_gram, y_cross, part_gram, part_cross, z_gram, z_cross,
    all_gram, all_cross, whole_gram, whole_cross, a_ref, spill_ref, x_ref,
    load_sem, core_s, core_r, y_s, y_r, zg_s, zg_r, zc_s, zc_r, bg_s, bg_r, bc_s, bc_r, yx_s, yx_r, yc_s, yc_r, x_s, x_r, f_s, f_r, n_s, n_r, l_s, l_r, p_s, p_r,
):
    samp, cell = lax.axis_index("samp"), lax.axis_index("cell")
    core = lax.rem(samp, 2)
    y = lax.rem(samp // 2, 4)
    z = samp // 8

    def at(zz, yy, cc, xx):
        return {"samp": (zz * 4 + yy) * 2 + cc, "cell": xx}

    def turn(v, d, n):
        return lax.rem(v + d, n)

    other = at(z, y, 1 - core, cell)
    far = (8, 7, 9, 6, 10, 5, 11, 4, 12, 3, 13, 2, 14, 1, 15)
    plane = [(dy, dx) for dy in (2, 1, 3, 0) for dx in (2, 1, 3, 0) if (dy, dx) != (0, 0)]
    close = (4, 3, 13, 2, 14, 1, 15)
    barrier = pltpu.get_barrier_semaphore()
    greet = [at(turn(z, d, 16), y, core, cell) for d in far]
    greet += [at(z, turn(y, dy, 4), core, turn(cell, dx, 4)) for dy, dx in plane]
    greet += [other] + [at(z, turn(y, d, 4), 1 - core, cell) for d in (2, 1, 3)]
    for device in greet:
        pl.semaphore_signal(barrier, inc=1, device_id=device, device_id_type=MESH)

    loads = [
        pltpu.make_async_copy(terms_hbm, terms_ref, load_sem.at[0]),
        pltpu.make_async_copy(points_hbm, points_ref, load_sem.at[1]),
        pltpu.make_async_copy(yields_hbm, yields_ref, load_sem.at[2]),
        pltpu.make_async_copy(group_hbm, group_ref, load_sem.at[3]),
    ]
    for copy in loads:
        copy.start()
    loads[0].wait()
    loads[1].wait()
    basis(terms_ref, points_ref, psi_ref)
    gram_quarter(cell, psi_ref, gram_ref, corner_ref)
    loads[2].wait()
    cross_ref[...] = jnp.dot(psi_ref[...], yields_ref[...], preferred_element_type=F32)
    loads[3].wait()
    pl.semaphore_wait(barrier, len(greet))

    sent = []

    def remote(src, dst, s, r, device):
        return pltpu.make_async_remote_copy(
            src_ref=src, dst_ref=dst, send_sem=s, recv_sem=r, device_id=device, device_id_type=MESH)

    def go(*args):
        copy = remote(*args)
        copy.start()
        sent.append(copy)
        return copy

    def arrive(copies):
        for copy in copies:
            copy.wait_recv()

    me = y * 2 + core
    mates = [
        (turn(y, dy, 4), 1 - core if flip else core)
        for dy, flip in ((2, 0), (2, 1), (1, 0), (1, 1), (3, 0), (3, 1), (0, 1))]
    near_ref[me] = corner_ref[tile(y * 8, 8)]
    near = [
        go(corner_ref.at[tile(yy * 8, 8)], near_ref.at[me], n_s.at[n], n_r.at[n], at(z, yy, cc, cell)) for n, (yy, cc) in enumerate(mates)]
    along_g = [
        go(gram_ref.at[tile(cc * 160 + yy * 40, 40)], y_gram.at[me], y_s.at[n], y_r.at[n], at(z, yy, cc, cell))
        for n, (yy, cc) in enumerate(mates)]
    along_c = [
        go(cross_ref.at[tile(yy * 128, 128), lanes(cc * 128, 128)], y_cross.at[me], y_s.at[7 + n], y_r.at[7 + n], at(z, yy, cc, cell))
        for n, (yy, cc) in enumerate(mates)]
    y_gram[me] = gram_ref[tile(core * 160 + y * 40, 40)]
    y_cross[me] = cross_ref[tile(y * 128, 128), lanes(core * 128, 128)]
    arrive(near)
    line_ref[z] = tree([near_ref[n] for n in range(8)])
    line = [go(line_ref.at[z], line_ref.at[z], l_s.at[d - 1], l_r.at[d - 1], at(turn(z, d, 16), y, core, cell)) for d in far]

    kind = lax.rem(z, 8)
    arrive(along_g)
    part_gram[...] = tree([y_gram[n] for n in range(8)])
    to_owner = []
    for v in range(5):
        for half in (0, 1):
            copy = remote(
                part_gram.at[8 * v:8 * v + 8], z_gram.at[z], zg_s.at[2 * v + half], zg_r.at[z], at(v + 8 * half, y, core, cell))
            to_owner.append((v + 8 * half, copy))
            pl.when(z != v + 8 * half)(copy.start)
    arrive(along_c)
    part_cross[...] = tree([y_cross[n] for n in range(8)])
    mine = tile(kind * 16, 16)
    z_cross[z] = part_cross[mine]
    z_c = [
        go(part_cross.at[tile(lax.rem(z + d, 8) * 16, 16)], z_cross.at[z], zc_s.at[d - 1], zc_r.at[d - 1], at(turn(z, d, 16), y, core, cell))
        for d in far]
    owned = tile(jnp.minimum(kind, 4) * 8, 8)
    back_g = [
        remote(all_gram.at[owned], all_gram.at[owned], bg_s.at[n], bg_r.at[jnp.minimum(kind, 4)], at(turn(z, d, 16), y, core, cell))
        for n, d in enumerate(close)]

    arrive(line)
    corner = tile(cell * 32 + y * 8, 8)
    first_ref[corner] = tree([line_ref[n] for n in range(16)])
    first = [
        go(first_ref.at[corner], first_ref.at[corner], p_s.at[n], p_r.at[n], at(z, turn(y, dy, 4), core, turn(cell, dx, 4)))
        for n, (dy, dx) in enumerate(plane)]

    @pl.when(kind < 5)
    def _():
        z_gram[z] = part_gram[owned]
        for d in range(1, 16):
            source = turn(z, d, 16)
            remote(part_gram.at[0:8], z_gram.at[source], zg_s.at[0], zg_r.at[source], other).wait_recv()
        all_gram[owned] = tree([z_gram[n] for n in range(16)])
        for copy in back_g:
            copy.start()

    arrive(z_c)
    all_cross[mine] = tree([z_cross[n] for n in range(16)])
    back_c = [
        go(all_cross.at[mine], all_cross.at[mine], bc_s.at[n], bc_r.at[n], at(turn(z, d, 16), y, core, cell))
        for n, d in enumerate(close)]

    rows = tile(core * 160 + y * 40, 40)
    half = tile(core * 160, 160)
    spot = tile(y * 128, 128)
    side = lanes(core * 128, 128)
    cells = whole_cross.shape[1]
    wide_g, wide_c = [], []

    def spread_gram():
        for v in range(5):
            apart = lax.rem(z + 16 - v, 8)
            pl.when(apart != 0)(remote(part_gram.at[0:8], all_gram.at[8 * v:8 * v + 8], zg_s.at[0], bg_r.at[v], other).wait_recv)
        for n, (dy, dx) in enumerate(plane):
            wide_g.append(go(
                all_gram, whole_gram.at[cell, rows], yx_s.at[n], yx_r.at[n], at(z, turn(y, dy, 4), core, turn(cell, dx, 4))))
        whole_gram[cell, rows] = all_gram[...]

    def spread_cross():
        arrive(back_c)
        for n, (yy, cc) in enumerate(mates):
            wide_c.append(go(all_cross, whole_cross.at[spot, side], yc_s.at[n], yc_r.at[n], at(z, yy, cc, cell)))
        whole_cross[spot, side] = all_cross[...]

    def take_gram():
        arrive(wide_g)
        pair_g = go(whole_gram.at[:, half], whole_gram.at[:, half], core_s.at[0], core_r.at[0], other)
        pair_g.wait_recv()
        place_gram(whole_gram, a_ref)

    def take_cross():
        arrive(wide_c)
        for i in range(4):
            a_ref[i, :, 512:512 + cells] = whole_cross[128 * i:128 * i + 128]

    arrive(first)
    column = cell * cells + core * 128
    own = lanes(cell * cells, cells)
    found = [None] * 4
    handed = []
    for b, x in eliminate(first_ref[...], a_ref, spill_ref, {0: {2: spread_gram, 11: spread_cross}}, {0: take_gram, 1: take_cross}):
        found[b] = x
        x_ref[b] = x
        for v in range(4):
            copy = remote(
                x_ref.at[b, 32 * v:32 * v + 32, side], coef_out.at[32 * b:32 * b + 32, lanes(column, 128)],
                x_s.at[4 * b + v], x_r.at[4 * b + cell], at(z, y, core, v))
            handed.append((v, copy))
            pl.when(cell != v)(copy.start)
        coef_out[32 * b:32 * b + 32, own] = x_ref[b, tile(cell * 32, 32), :]

    sums = []
    for quarter in range(4):
        for low in (0, 2):
            value = None
            for b in (low, low + 1):
                sq = found[b][32 * quarter:32 * quarter + 32] * found[b][32 * quarter:32 * quarter + 32]
                if quarter == 0 and b == 0:
                    sq = jnp.where(lax.broadcasted_iota(jnp.int32, sq.shape, 0) == 0, 0.0, sq)
                value = sq if value is None else value + sq
            sums.append(jnp.sum(value, axis=0, keepdims=True))
    total = sums[0]
    for s in sums[1:]:
        total = total + s
    for g in range(GROUPS):
        part = jnp.zeros_like(total)
        for b in range(8):
            part = part + jnp.where(group_ref[b] == g, sums[b], 0.0)
        share_out[g:g + 1] = part / total

    for copy in sent:
        copy.wait_send()
    for v, copy in to_owner:
        pl.when(z != v)(copy.wait_send)

    @pl.when(kind < 5)
    def _():
        for copy in back_g:
            copy.wait_send()

    passed = []
    for n, blocks in enumerate(((3, 2, 1), (0,))):
        piece_rows = slice(32 * min(blocks), 32 * max(blocks) + 32)
        for d in (1, 3, 2):
            source = turn(cell, d, 4)
            place = lanes(source * cells + core * 128, 128)
            for b in blocks:
                remote(x_ref.at[0, 0:32, side], coef_out.at[32 * b:32 * b + 32, place], x_s.at[0], x_r.at[4 * b + source], other).wait_recv()
            piece = coef_out.at[piece_rows, place]
            copy = remote(piece, piece, f_s.at[3 * n + d - 1], f_r.at[3 * n + d - 1], other)
            copy.start()
            passed.append(copy)
    arrive(passed)
    for copy in passed:
        copy.wait_send()
    for v, copy in handed:
        pl.when(cell != v)(copy.wait_send)


def fit(points, yields, term_index, block_group):
    hbm = pl.BlockSpec(memory_space=pltpu.HBM)
    vmem = pl.BlockSpec(memory_space=pltpu.VMEM)
    params, samples = points.shape
    cells = yields.shape[1]
    dma = pltpu.SemaphoreType.DMA

    def f32(*shape):
        return pltpu.VMEM(shape, F32)

    points, yields, terms, block_group = (
        pltpu.with_memory_space_constraint(v, pltpu.HBM) for v in (points, yields, term_index.T, block_group))
    return pl.pallas_call(
        fit_kernel,
        out_shape=(jax.ShapeDtypeStruct((TERMS // 4, cells * 4), F32), jax.ShapeDtypeStruct((GROUPS, cells), F32)),
        in_specs=[hbm] * 4,
        out_specs=(vmem, vmem),
        scratch_shapes=[
            f32(params, samples), pltpu.VMEM((samples, cells), BF16), pltpu.VMEM((2, TERMS), jnp.int32), pltpu.SMEM((8,), jnp.int32),
            pltpu.VMEM((TERMS, samples), BF16), f32(TERMS, cells), f32(320, 128),
            f32(32, 128), f32(8, 8, 128), f32(16, 8, 128), f32(128, 128),
            f32(8, 40, 128), f32(8, 128, 128), f32(40, 128), f32(128, 128),
            f32(16, 8, 128), f32(16, 16, 128), f32(40, 128), f32(128, 128), f32(4, 320, 128), f32(TERMS, cells),
            f32(4, 128, 512 + cells), f32(18, 8, 128), f32(4, 128, cells),
            dma((4,)), dma((1,)), dma((1,)), dma((14,)), dma((14,)), dma((10,)), dma((16,)), dma((15,)), dma((15,)),
            dma((7,)), dma((5,)), dma((7,)), dma((7,)), dma((15,)), dma((15,)), dma((7,)), dma((7,)),
            dma((16,)), dma((16,)), dma((6,)), dma((6,)), dma((7,)), dma((7,)), dma((15,)), dma((15,)), dma((15,)), dma((15,)),
        ],
        compiler_params=pltpu.CompilerParams(collective_id=0, has_side_effects=True, vmem_limit_bytes=48 << 20),
        name="fit",
    )(points, yields, terms, block_group)


def finish_kernel(scale, coef_ref, share_ref, coef_hbm, share_hbm, scaled_ref, sem):
    copies = [pltpu.make_async_copy(share_ref, share_hbm, sem.at[4])]
    copies[0].start()
    for n in range(4):
        rows = slice(32 * n, 32 * n + 32)
        scaled_ref[rows] = coef_ref[rows] * scale
        copies.append(pltpu.make_async_copy(scaled_ref.at[rows], coef_hbm.at[rows], sem.at[n]))
        copies[-1].start()
    for copy in copies:
        copy.wait()


def finish(coef, share, scale):
    hbm = pl.BlockSpec(memory_space=pltpu.HBM)
    vmem = pl.BlockSpec(memory_space=pltpu.VMEM)
    return pl.pallas_call(
        functools.partial(finish_kernel, scale),
        out_shape=(jax.ShapeDtypeStruct(coef.shape, F32), jax.ShapeDtypeStruct(share.shape, F32)),
        in_specs=[vmem, vmem],
        out_specs=(hbm, hbm),
        scratch_shapes=[pltpu.VMEM(coef.shape, F32), pltpu.SemaphoreType.DMA((5,))],
        compiler_params=pltpu.CompilerParams(vmem_limit_bytes=4 << 20),
        name="finish",
    )(coef, share)


def on_device(points, yields, term_index, block_group):
    coef, sobol = fit(points, yields, term_index, block_group)
    return finish(coef, sobol, float(points.shape[1] * lax.axis_size("samp")) ** 0.5)


def solution(mesh):
    placed = (P(None, "samp"), P("samp", "cell"), P(), P())
    return jax.shard_map(
        on_device,
        mesh=mesh,
        in_specs=placed,
        out_specs=(P("cell", None), P(None, "cell")),
        check_vma=False,
    )
```

```python
import functools

import jax
import jax.numpy as jnp
from jax import lax
from jax.experimental import pallas as pl
from jax.experimental.pallas import tpu as pltpu
from jax.sharding import PartitionSpec as P

GROUPS = 8
TERMS = 512
MESH = pl.DeviceIdType.MESH
F32 = jnp.float32
BF16 = jnp.bfloat16


def tile(start, size):
    return pl.ds(pl.multiple_of(start, 8), size)


def lanes(start, size):
    return pl.ds(pl.multiple_of(start, 128), size)


def basis(terms_ref, points_ref, psi_ref):
    params, samples = points_ref.shape
    width = 3 * params
    place = lax.broadcasted_iota(jnp.int32, (256, TERMS), 0)
    order = [128 * quarter + 32 * block for block in range(4) for quarter in range(4)]

    def pick(column):
        degree = column & 3
        target = (degree - 1) * params + (column >> 2)
        hit = (place == target) | (place == target + width) | (place == target + 2 * width)
        chosen = jnp.where(degree == 0, (place == 3 * width).astype(F32), hit.astype(F32))
        straight = chosen.T
        return jnp.concatenate([straight[start:start + 32] for start in order], axis=0).astype(BF16)

    pick_a = pick(terms_ref[0:1, :])
    pick_b = pick(terms_ref[1:2, :])
    step = 512
    for start in range(0, samples, step):
        xs = points_ref[:, start:start + step]
        first = 1.7320508075688772 * xs
        second = 2.23606797749979 * (1.5 * xs * xs - 0.5)
        third = 2.6457513110645907 * (2.5 * xs * xs * xs - 1.5 * xs)
        degrees = jnp.concatenate([first, second, third], axis=0)
        high = degrees.astype(BF16).astype(F32)
        rest = degrees - high
        middle = rest.astype(BF16).astype(F32)
        low = rest - middle
        table = jnp.concatenate(
            [high, middle, low, jnp.ones((8, step), F32), jnp.zeros((256 - 3 * width - 8, step), F32)], axis=0
        ).astype(BF16)
        left = jnp.dot(pick_a, table, preferred_element_type=F32)
        right = jnp.dot(pick_b, table, preferred_element_type=F32)
        psi_ref[:, start:start + step] = (left * right).astype(BF16)


def gram_quarter(cell, psi_ref, gram_ref, corner_ref):
    corner_ref[...] = lax.dot_general(
        psi_ref[pl.ds(pl.multiple_of(cell * 32, 32), 32), :], psi_ref[0:128, :], (((1,), (1,)), ((), ())), preferred_element_type=F32)
    low_half = cell < 2
    spots = (
        (0, 128, cell * 128, cell * 128),
        (128, 128, jnp.where(cell == 3, 0, cell * 128), jnp.minimum(cell + 1, 3) * 128),
        (256, 64, jnp.where(low_half, cell * 128, cell * 128 - 192), jnp.where(low_half, cell * 128 + 256, cell * 128)),
    )
    for place, rows, a, b in spots:
        one = psi_ref[pl.ds(pl.multiple_of(a, 64), rows), :]
        two = psi_ref[pl.ds(pl.multiple_of(b, 128), 128), :]
        gram_ref[place:place + rows, :] = lax.dot_general(one, two, (((1,), (1,)), ((), ())), preferred_element_type=F32)


def full(row):
    return jnp.broadcast_to(row, (8, 128))


def tree(terms):
    terms = list(terms)
    while len(terms) > 1:
        terms = [terms[i] + terms[i + 1] for i in range(0, len(terms), 2)]
    return terms[0]


def parts(v):
    a = v.astype(BF16)
    rest = v - a.astype(F32)
    b = rest.astype(BF16)
    return a, b, (rest - b.astype(F32)).astype(BF16)


def as_left(v, axis):
    a, b, c = parts(v)
    return jnp.concatenate([a, a, b, b, a, c], axis=axis)


def as_right(v):
    a, b, c = parts(v)
    return jnp.concatenate([a, b, a, b, c, a], axis=0)


def mul(left, right, axis):
    return lax.dot_general(left, right, (((axis,), (0,)), ((), ())), preferred_element_type=F32)


def sweep_rows(rows, p, lane, sub, spill):
    pivot = rows[p]
    at = 8 * p
    inside = (lane >= at) & (lane < at + 8)
    target = jnp.where(inside, jnp.where(lane - at == sub, 1.0, 0.0), -pivot)
    base = 9 * (p % 2)
    for j in range(8):
        spill[base + j] = full(pivot[:, at + j:at + j + 1])
    spill[base + 8] = target

    def row(k, i):
        return spill[base + k, pl.ds(i, 8, stride=0), :]

    m = [[None] * 8 for _ in range(8)]
    for j in range(8):
        for i in range(j + 1):
            m[i][j] = row(j, i)
    for k in range(8):
        r = 1.0 / m[k][k]
        old = [m[min(j, k)][max(j, k)] for j in range(8)]
        t = [None if j == k else old[j] * r for j in range(8)]
        for j in range(8):
            for i in range(j + 1):
                if i != k and j != k:
                    m[i][j] = m[i][j] - old[i] * t[j]
        for j in range(8):
            if j != k:
                m[min(j, k)][max(j, k)] = t[j]
        m[k][k] = -r
    source = [row(8, i) for i in range(8)]
    wide = [tree([m[min(i, j)][max(i, j)] * source[i] for i in range(8)]) for j in range(8)]
    out = list(rows)
    near = [q for q in (p + 1, p + 2) if q < 16]
    for q in near:
        out[q] = jnp.where(inside, 0.0, rows[q]) - tree([full(rows[q][:, at + j:at + j + 1]) * wide[j] for j in range(8)])
    packed = wide[7]
    for j in range(7):
        packed = jnp.where(sub == j, wide[j], packed)
    u = [v.astype(F32) for v in parts(pivot)]
    w = [v.astype(F32) for v in parts(packed)]
    left = jnp.concatenate([u[0], u[0], u[1], u[1], u[0], u[2]], axis=0).astype(BF16)
    right = jnp.concatenate([w[0], w[1], w[0], w[1], w[2], w[0]], axis=0).astype(BF16)
    change = mul(left, right, 0)
    for q in range(16):
        if q != p and q not in near:
            out[q] = jnp.where(inside, 0.0, rows[q]) - change[8 * q:8 * q + 8]
    out[p] = packed
    return out


def invert(block, spill, between):
    lane = lax.broadcasted_iota(jnp.int32, (8, 128), 1)
    sub = lax.broadcasted_iota(jnp.int32, (8, 128), 0)
    rows = [block[8 * i:8 * i + 8] for i in range(16)]
    for p in range(16):
        if p in between:
            between[p]()
        rows = sweep_rows(rows, p, lane, sub, spill)
    return -jnp.concatenate(rows, axis=0)


def eliminate(corner, a_ref, spill, between, after):
    end = a_ref.shape[2]
    diag = corner
    kept = []

    def forward(b):
        right = as_right(a_ref[b, :, 512:end])
        for i in range(b + 1, 4):
            a_ref[i, :, 512:end] -= mul(as_left(a_ref[b, :, 128 * i:128 * i + 128], 0), right, 0)
        a_ref[b, :, 512:end] = mul(kept[b], right, 1)

    def trail(b, s1):
        cut = 128 * b + 256
        s2 = a_ref[b, :, cut:512]
        w2 = mul(kept[b], as_right(s2), 1)
        a_ref[b, :, cut:512] = w2
        right = as_right(w2)
        a_ref[b + 1, :, cut:512] -= mul(as_left(s1, 0), right, 0)
        for i in range(b + 2, 4):
            left = as_left(s2[:, 128 * i - cut:128 * i - cut + 128], 0)
            a_ref[i, :, 128 * i:512] -= mul(left, right[:, 128 * i - cut:], 0)

    for b in range(4):
        steps = dict(between.get(b, {}))
        if b in (1, 2):
            steps[2] = functools.partial(trail, b - 1, s1)
        if b == 2:
            steps[6] = functools.partial(forward, 0)
        if b == 3:
            steps[2] = functools.partial(forward, 1)
            steps[7] = functools.partial(forward, 2)
        inverse = invert(diag, spill, steps)
        after.get(b, lambda: None)()
        kept.append(as_left(inverse, 1))
        begin = 128 * b + 128
        if b < 3:
            s1 = a_ref[b, :, begin:begin + 128]
            w1 = mul(kept[b], as_right(s1), 1)
            diag = a_ref[b + 1, :, begin:begin + 128] - mul(as_left(s1, 0), as_right(w1), 0)
            a_ref[b, :, begin:begin + 128] = w1
    forward(3)
    for b in (3, 2, 1, 0):
        x = a_ref[b, :, 512:end]
        yield b, x
        right = as_right(x)
        for i in range(b - 1, -1, -1):
            a_ref[i, :, 512:end] -= mul(as_left(a_ref[i, :, 128 * b:128 * b + 128], 1), right, 1)


def place_gram(gram_ref, a_ref):
    for b in range(1, 4):
        a_ref[b, :, 128 * b:128 * b + 128] = gram_ref[b, 0:128]
    for b in range(3):
        a_ref[b, :, 128 * b + 128:128 * b + 256] = gram_ref[b, 128:256]
    a_ref[0, :, 384:512] = gram_ref[3, 128:256]
    for b in range(2):
        a_ref[b, 0:64, 128 * b + 256:128 * b + 384] = gram_ref[b, 256:320]
        a_ref[b, 64:128, 128 * b + 256:128 * b + 384] = gram_ref[b + 2, 256:320]


def fit_kernel(
    points_hbm, yields_hbm, terms_hbm, group_hbm, coef_out, share_out,
    points_ref, yields_ref, terms_ref, group_ref, psi_ref, cross_ref, gram_ref, corner_ref, near_ref, line_ref, first_ref,
    y_gram, y_cross, part_gram, part_cross, z_gram, z_cross,
    all_gram, all_cross, whole_gram, whole_cross, a_ref, spill_ref, x_ref,
    load_sem, core_s, core_r, y_s, y_r, zg_s, zg_r, zc_s, zc_r, bg_s, bg_r, bc_s, bc_r, yx_s, yx_r, yc_s, yc_r, x_s, x_r, f_s, f_r, n_s, n_r, l_s, l_r, p_s, p_r,
):
    samp, cell = lax.axis_index("samp"), lax.axis_index("cell")
    core = lax.rem(samp, 2)
    y = lax.rem(samp // 2, 4)
    z = samp // 8

    def at(zz, yy, cc, xx):
        return {"samp": (zz * 4 + yy) * 2 + cc, "cell": xx}

    def turn(v, d, n):
        return lax.rem(v + d, n)

    other = at(z, y, 1 - core, cell)
    far = (8, 7, 9, 6, 10, 5, 11, 4, 12, 3, 13, 2, 14, 1, 15)
    plane = [(dy, dx) for dy in (2, 1, 3, 0) for dx in (2, 1, 3, 0) if (dy, dx) != (0, 0)]
    close = (4, 3, 13, 2, 14, 1, 15)
    barrier = pltpu.get_barrier_semaphore()
    greet = [at(turn(z, d, 16), y, core, cell) for d in far]
    greet += [at(z, turn(y, dy, 4), core, turn(cell, dx, 4)) for dy, dx in plane]
    greet += [other] + [at(z, turn(y, d, 4), 1 - core, cell) for d in (2, 1, 3)]
    for device in greet:
        pl.semaphore_signal(barrier, inc=1, device_id=device, device_id_type=MESH)

    loads = [
        pltpu.make_async_copy(terms_hbm, terms_ref, load_sem.at[0]),
        pltpu.make_async_copy(points_hbm, points_ref, load_sem.at[1]),
        pltpu.make_async_copy(yields_hbm, yields_ref, load_sem.at[2]),
        pltpu.make_async_copy(group_hbm, group_ref, load_sem.at[3]),
    ]
    for copy in loads:
        copy.start()
    loads[0].wait()
    loads[1].wait()
    basis(terms_ref, points_ref, psi_ref)
    gram_quarter(cell, psi_ref, gram_ref, corner_ref)
    loads[2].wait()
    cross_ref[...] = jnp.dot(psi_ref[...], yields_ref[...], preferred_element_type=F32)
    loads[3].wait()
    pl.semaphore_wait(barrier, len(greet))

    sent = []

    def remote(src, dst, s, r, device):
        return pltpu.make_async_remote_copy(
            src_ref=src, dst_ref=dst, send_sem=s, recv_sem=r, device_id=device, device_id_type=MESH)

    def go(*args):
        copy = remote(*args)
        copy.start()
        sent.append(copy)
        return copy

    def arrive(copies):
        for copy in copies:
            copy.wait_recv()

    me = y * 2 + core
    mates = [
        (turn(y, dy, 4), 1 - core if flip else core)
        for dy, flip in ((2, 0), (2, 1), (1, 0), (1, 1), (3, 0), (3, 1), (0, 1))]
    near_ref[me] = corner_ref[tile(y * 8, 8)]
    near = [
        go(corner_ref.at[tile(yy * 8, 8)], near_ref.at[me], n_s.at[n], n_r.at[n], at(z, yy, cc, cell)) for n, (yy, cc) in enumerate(mates)]
    along_g = [
        go(gram_ref.at[tile(cc * 160 + yy * 40, 40)], y_gram.at[me], y_s.at[n], y_r.at[n], at(z, yy, cc, cell))
        for n, (yy, cc) in enumerate(mates)]
    along_c = [
        go(cross_ref.at[tile(yy * 128, 128), lanes(cc * 128, 128)], y_cross.at[me], y_s.at[7 + n], y_r.at[7 + n], at(z, yy, cc, cell))
        for n, (yy, cc) in enumerate(mates)]
    y_gram[me] = gram_ref[tile(core * 160 + y * 40, 40)]
    y_cross[me] = cross_ref[tile(y * 128, 128), lanes(core * 128, 128)]
    arrive(near)
    line_ref[z] = tree([near_ref[n] for n in range(8)])
    line = [go(line_ref.at[z], line_ref.at[z], l_s.at[d - 1], l_r.at[d - 1], at(turn(z, d, 16), y, core, cell)) for d in far]

    kind = lax.rem(z, 8)
    arrive(along_g)
    part_gram[...] = tree([y_gram[n] for n in range(8)])
    to_owner = []
    for v in range(5):
        for half in (0, 1):
            copy = remote(
                part_gram.at[8 * v:8 * v + 8], z_gram.at[z], zg_s.at[2 * v + half], zg_r.at[z], at(v + 8 * half, y, core, cell))
            to_owner.append((v + 8 * half, copy))
            pl.when(z != v + 8 * half)(copy.start)
    arrive(along_c)
    part_cross[...] = tree([y_cross[n] for n in range(8)])
    mine = tile(kind * 16, 16)
    z_cross[z] = part_cross[mine]
    z_c = [
        go(part_cross.at[tile(lax.rem(z + d, 8) * 16, 16)], z_cross.at[z], zc_s.at[d - 1], zc_r.at[d - 1], at(turn(z, d, 16), y, core, cell))
        for d in far]
    owned = tile(jnp.minimum(kind, 4) * 8, 8)
    back_g = [
        remote(all_gram.at[owned], all_gram.at[owned], bg_s.at[n], bg_r.at[jnp.minimum(kind, 4)], at(turn(z, d, 16), y, core, cell))
        for n, d in enumerate(close)]

    arrive(line)
    corner = tile(cell * 32 + y * 8, 8)
    first_ref[corner] = tree([line_ref[n] for n in range(16)])
    first = [
        go(first_ref.at[corner], first_ref.at[corner], p_s.at[n], p_r.at[n], at(z, turn(y, dy, 4), core, turn(cell, dx, 4)))
        for n, (dy, dx) in enumerate(plane)]

    @pl.when(kind < 5)
    def _():
        z_gram[z] = part_gram[owned]
        for d in range(1, 16):
            source = turn(z, d, 16)
            remote(part_gram.at[0:8], z_gram.at[source], zg_s.at[0], zg_r.at[source], other).wait_recv()
        all_gram[owned] = tree([z_gram[n] for n in range(16)])
        for copy in back_g:
            copy.start()

    arrive(z_c)
    all_cross[mine] = tree([z_cross[n] for n in range(16)])
    back_c = [
        go(all_cross.at[mine], all_cross.at[mine], bc_s.at[n], bc_r.at[n], at(turn(z, d, 16), y, core, cell))
        for n, d in enumerate(close)]

    rows = tile(core * 160 + y * 40, 40)
    half = tile(core * 160, 160)
    spot = tile(y * 128, 128)
    side = lanes(core * 128, 128)
    cells = whole_cross.shape[1]
    wide_g, wide_c = [], []

    def spread_gram():
        for v in range(5):
            apart = lax.rem(z + 16 - v, 8)
            pl.when(apart != 0)(remote(part_gram.at[0:8], all_gram.at[8 * v:8 * v + 8], zg_s.at[0], bg_r.at[v], other).wait_recv)
        for n, (dy, dx) in enumerate(plane):
            wide_g.append(go(
                all_gram, whole_gram.at[cell, rows], yx_s.at[n], yx_r.at[n], at(z, turn(y, dy, 4), core, turn(cell, dx, 4))))
        whole_gram[cell, rows] = all_gram[...]

    def spread_cross():
        arrive(back_c)
        for n, (yy, cc) in enumerate(mates):
            wide_c.append(go(all_cross, whole_cross.at[spot, side], yc_s.at[n], yc_r.at[n], at(z, yy, cc, cell)))
        whole_cross[spot, side] = all_cross[...]

    def take_gram():
        arrive(wide_g)
        pair_g = go(whole_gram.at[:, half], whole_gram.at[:, half], core_s.at[0], core_r.at[0], other)
        pair_g.wait_recv()
        place_gram(whole_gram, a_ref)

    def take_cross():
        arrive(wide_c)
        for i in range(4):
            a_ref[i, :, 512:512 + cells] = whole_cross[128 * i:128 * i + 128]

    spread_gram()
    arrive(first)
    column = cell * cells + core * 128
    own = lanes(cell * cells, cells)
    found = [None] * 4
    handed = []
    for b, x in eliminate(first_ref[...], a_ref, spill_ref, {0: {11: spread_cross}, 2: {5: take_cross}}, {0: take_gram}):
        found[b] = x
        x_ref[b] = x
        for v in range(4):
            copy = remote(
                x_ref.at[b, 32 * v:32 * v + 32, side], coef_out.at[32 * b:32 * b + 32, lanes(column, 128)],
                x_s.at[4 * b + v], x_r.at[4 * b + cell], at(z, y, core, v))
            handed.append((v, copy))
            pl.when(cell != v)(copy.start)
        coef_out[32 * b:32 * b + 32, own] = x_ref[b, tile(cell * 32, 32), :]

    sums = []
    for quarter in range(4):
        for low in (0, 2):
            value = None
            for b in (low, low + 1):
                sq = found[b][32 * quarter:32 * quarter + 32] * found[b][32 * quarter:32 * quarter + 32]
                if quarter == 0 and b == 0:
                    sq = jnp.where(lax.broadcasted_iota(jnp.int32, sq.shape, 0) == 0, 0.0, sq)
                value = sq if value is None else value + sq
            sums.append(jnp.sum(value, axis=0, keepdims=True))
    total = sums[0]
    for s in sums[1:]:
        total = total + s
    for g in range(GROUPS):
        part = jnp.zeros_like(total)
        for b in range(8):
            part = part + jnp.where(group_ref[b] == g, sums[b], 0.0)
        share_out[g:g + 1] = part / total

    for copy in sent:
        copy.wait_send()
    for v, copy in to_owner:
        pl.when(z != v)(copy.wait_send)

    @pl.when(kind < 5)
    def _():
        for copy in back_g:
            copy.wait_send()

    passed = []
    for n, blocks in enumerate(((3, 2, 1), (0,))):
        piece_rows = slice(32 * min(blocks), 32 * max(blocks) + 32)
        for d in (1, 3, 2):
            source = turn(cell, d, 4)
            place = lanes(source * cells + core * 128, 128)
            for b in blocks:
                remote(x_ref.at[0, 0:32, side], coef_out.at[32 * b:32 * b + 32, place], x_s.at[0], x_r.at[4 * b + source], other).wait_recv()
            piece = coef_out.at[piece_rows, place]
            copy = remote(piece, piece, f_s.at[3 * n + d - 1], f_r.at[3 * n + d - 1], other)
            copy.start()
            passed.append(copy)
    arrive(passed)
    for copy in passed:
        copy.wait_send()
    for v, copy in handed:
        pl.when(cell != v)(copy.wait_send)


def fit(points, yields, term_index, block_group):
    hbm = pl.BlockSpec(memory_space=pltpu.HBM)
    vmem = pl.BlockSpec(memory_space=pltpu.VMEM)
    params, samples = points.shape
    cells = yields.shape[1]
    dma = pltpu.SemaphoreType.DMA

    def f32(*shape):
        return pltpu.VMEM(shape, F32)

    points, yields, terms, block_group = (
        pltpu.with_memory_space_constraint(v, pltpu.HBM) for v in (points, yields, term_index.T, block_group))
    return pl.pallas_call(
        fit_kernel,
        out_shape=(jax.ShapeDtypeStruct((TERMS // 4, cells * 4), F32), jax.ShapeDtypeStruct((GROUPS, cells), F32)),
        in_specs=[hbm] * 4,
        out_specs=(vmem, vmem),
        scratch_shapes=[
            f32(params, samples), pltpu.VMEM((samples, cells), BF16), pltpu.VMEM((2, TERMS), jnp.int32), pltpu.SMEM((8,), jnp.int32),
            pltpu.VMEM((TERMS, samples), BF16), f32(TERMS, cells), f32(320, 128),
            f32(32, 128), f32(8, 8, 128), f32(16, 8, 128), f32(128, 128),
            f32(8, 40, 128), f32(8, 128, 128), f32(40, 128), f32(128, 128),
            f32(16, 8, 128), f32(16, 16, 128), f32(40, 128), f32(128, 128), f32(4, 320, 128), f32(TERMS, cells),
            f32(4, 128, 512 + cells), f32(18, 8, 128), f32(4, 128, cells),
            dma((4,)), dma((1,)), dma((1,)), dma((14,)), dma((14,)), dma((10,)), dma((16,)), dma((15,)), dma((15,)),
            dma((7,)), dma((5,)), dma((7,)), dma((7,)), dma((15,)), dma((15,)), dma((7,)), dma((7,)),
            dma((16,)), dma((16,)), dma((6,)), dma((6,)), dma((7,)), dma((7,)), dma((15,)), dma((15,)), dma((15,)), dma((15,)),
        ],
        compiler_params=pltpu.CompilerParams(collective_id=0, has_side_effects=True, vmem_limit_bytes=48 << 20),
        name="fit",
    )(points, yields, terms, block_group)


def finish_kernel(scale, coef_ref, share_ref, coef_hbm, share_hbm, scaled_ref, sem):
    copies = [pltpu.make_async_copy(share_ref, share_hbm, sem.at[4])]
    copies[0].start()
    for n in range(4):
        rows = slice(32 * n, 32 * n + 32)
        scaled_ref[rows] = coef_ref[rows] * scale
        copies.append(pltpu.make_async_copy(scaled_ref.at[rows], coef_hbm.at[rows], sem.at[n]))
        copies[-1].start()
    for copy in copies:
        copy.wait()


def finish(coef, share, scale):
    hbm = pl.BlockSpec(memory_space=pltpu.HBM)
    vmem = pl.BlockSpec(memory_space=pltpu.VMEM)
    return pl.pallas_call(
        functools.partial(finish_kernel, scale),
        out_shape=(jax.ShapeDtypeStruct(coef.shape, F32), jax.ShapeDtypeStruct(share.shape, F32)),
        in_specs=[vmem, vmem],
        out_specs=(hbm, hbm),
        scratch_shapes=[pltpu.VMEM(coef.shape, F32), pltpu.SemaphoreType.DMA((5,))],
        compiler_params=pltpu.CompilerParams(vmem_limit_bytes=4 << 20),
        name="finish",
    )(coef, share)


def on_device(points, yields, term_index, block_group):
    coef, sobol = fit(points, yields, term_index, block_group)
    return finish(coef, sobol, float(points.shape[1] * lax.axis_size("samp")) ** 0.5)


def solution(mesh):
    placed = (P(None, "samp"), P("samp", "cell"), P(), P())
    return jax.shard_map(
        on_device,
        mesh=mesh,
        in_specs=placed,
        out_specs=(P("cell", None), P(None, "cell")),
        check_vma=False,
    )
```
